256 devices in a mesh: bus: 32 (over x, z), case: 8 (over y, core).
Axes of the slice: x: 4, y: 4, z: 8, core: 2. Of those that a mesh axis runs over, the one named last changes fastest.
Arguments:
- z_columns: float32 [32768, 1024], P('bus')
- resident_bus: int32 [1024], replicated, may hold values from 0 to 32767, as said below
- fault_col: int32 [4096], P('case'), may hold values from 0 to 1023
- switch_cols: int32 [4096, 2], P('case'), may hold values from 0 to 1023, as said below
- tie_x: float32 [4096], P('case'), may hold values from 0.5 to 2
- fault_z: float32 [4096], P('case'), may hold values from 0.5 to 2
- boundary_send: int32 [32, 2, 128], replicated, may hold values from 0 to 1023, as said below
- branch_ends: int32 [49152, 2], P('bus'), may hold values from 0 to 1279, as said below
- branch_x: float32 [49152], P('bus'), may hold values from 0.01 to 0.05
- pickup: float32 [49152], P('bus'), may hold values from 0.2 to 1.5
- tds: float32 [49152], P('bus'), may hold values from 0.05 to 0.5
- curve: int32 [49152], P('bus'), may hold values from 0 to 2
Outputs:
- voltage: float32 [32768, 4096], P('bus', 'case')
- relay_rate: float32 [49152, 4096], P('bus', 'case')
- worst_rate: float32 [49152], P('bus')
The draws below stay inside these ranges and needn't reach their ends.
Inputs may be any that keep to these rules, and one draw needn't show every extreme that they name: `resident_bus`: distinct bus ids. `switch_cols`: the two columns of a case differ. `boundary_send`: rows sent to the lower block lie among the first 256 rows, rows sent to the upper block among the last 256; each block's live slots come first and hold distinct rows, padding repeats the first slot's row; the first block sends nothing down and the last nothing up; some block fills all 128 slots. `branch_ends`: a to slot of 1024 or more points at a live slot of the neighbour's block; the first block never uses the lower slots, the last never the upper ones; a local to row differs from the from row.
All inputs are finite; a program needn't handle non-finite values.
Results may differ from the reference program's by a relative error of at most 0.000049.
Values sent between devices are 32-bit elements; how exact they have to be, the bound alone decides.
A program may use at most 64 MiB of HBM per device.

```python
import math
import jax
import jax.numpy as jnp
from jax import lax

BUS_DEV = 1024
K = 1024
CASE_DEV = 512
BR_DEV = 1536
HB = 128
RIM = 256
NB = 32768
NBR = 49152
CASES = 4096
N_BUS = 32


def resident_ids(key):
    return jax.random.permutation(jax.random.fold_in(key, 11), NB)[:K].astype(jnp.int32)


def draw_resident_bus(key, part):
    return resident_ids(key)


def draw_z_columns(key, part):
    resident = resident_ids(key)
    noise_key = jax.random.fold_in(key, 12)
    noise = jnp.clip(0.04 * jax.random.normal(noise_key, (NB, K), jnp.float32), -0.24, 0.24)
    diagonal = jax.random.uniform(jax.random.fold_in(key, 13), (K,), jnp.float32, 2.0, 4.0)
    return noise.at[resident, jnp.arange(K)].add(diagonal)


def draw_switch_cols(key, part):
    first_col = jax.random.randint(jax.random.fold_in(key, 21), (CASES,), 0, K)
    offset_col = jax.random.randint(jax.random.fold_in(key, 22), (CASES,), 1, K)
    return jnp.stack([first_col, (first_col + offset_col) % K], axis=1).astype(jnp.int32)


def topology(key):
    shards = NB // BUS_DEV
    counts = jax.random.randint(jax.random.fold_in(key, 31), (shards, 2), HB // 2, HB + 1)
    counts = counts.at[1, 0].set(HB).at[0, 1].set(HB).at[0, 0].set(0).at[shards - 1, 1].set(0)
    scores = jax.random.randint(jax.random.fold_in(key, 32), (shards, 2, RIM), 0, 1048576) * RIM + jnp.arange(RIM, dtype=jnp.int32)
    chosen = jnp.argsort(scores, axis=-1)[..., :HB].astype(jnp.int32)
    chosen = chosen + jnp.array([0, BUS_DEV - RIM], jnp.int32)[None, :, None]
    slot_ids = jnp.arange(HB, dtype=jnp.int32)[None, None, :]
    send_rows = jnp.where(slot_ids < counts[:, :, None], chosen, chosen[..., :1])
    branch = jnp.arange(NBR, dtype=jnp.int32)
    owner = branch // BR_DEV
    position = branch % BR_DEV
    anchor = jax.random.randint(jax.random.fold_in(key, 33), (NBR,), 0, BUS_DEV)
    local_to = (anchor + jax.random.randint(jax.random.fold_in(key, 34), (NBR,), 1, BUS_DEV)) % BUS_DEV
    draw_r = jax.random.randint(jax.random.fold_in(key, 35), (NBR,), 0, 1048576)
    go_lower = (position % 2 == 0) & (owner > 0) | (owner == shards - 1)
    lower_count = counts[jnp.maximum(owner - 1, 0), 1]
    upper_count = counts[jnp.minimum(owner + 1, shards - 1), 0]
    lower_slot = BUS_DEV + draw_r % jnp.maximum(lower_count, 1)
    upper_slot = BUS_DEV + HB + draw_r % jnp.maximum(upper_count, 1)
    target = jnp.where(position < BR_DEV // 4, jnp.where(go_lower, lower_slot, upper_slot), local_to)
    return (send_rows.astype(jnp.int32), jnp.stack([anchor, target], axis=1).astype(jnp.int32))


def draw_boundary_send(key, part):
    return topology(key)[0]


def draw_branch_ends(key, part):
    return topology(key)[1]


def place_ends(result, stream_key, least, top_value):
    spot = [jax.random.randint(jax.random.fold_in(stream_key, axis), (), 0, length) for axis, length in enumerate(result.shape)]
    widest = result.shape.index(max(result.shape))
    beside = spot[:widest] + [(spot[widest] + 1) % result.shape[widest]] + spot[widest + 1:]
    return result.at[tuple(spot)].set(least).at[tuple(beside)].set(top_value)


def block_scale(stream_key, shape, split, smallest, largest):
    gain = 1.0
    for dim, parts in split:
        steps = jax.random.uniform(jax.random.fold_in(jax.random.fold_in(stream_key, 6), dim), (parts,), jnp.float32, smallest / len(split), largest / len(split))
        gain = gain * jnp.repeat(jnp.exp(steps), shape[dim] // parts).reshape((-1,) + (1,) * (len(shape) - 1 - dim))
    return gain


def setup_inputs(seed: int = 0) -> dict:
    keys = jax.random.split(jax.random.key(seed), 13)
    return {
        "z_columns": draw_z_columns(jax.random.fold_in(keys[12], 71), 0),
        "resident_bus": draw_resident_bus(jax.random.fold_in(keys[12], 71), 0),
        "fault_col": place_ends(jax.random.randint(keys[2], (CASES,), 0, K), jax.random.fold_in(keys[2], 1), 0, K - 1).astype(jnp.int32),
        "switch_cols": draw_switch_cols(jax.random.fold_in(keys[12], 71), 0),
        "tie_x": jnp.clip(jnp.exp(math.log(2.0) - 1.3862944 * jax.random.uniform(keys[4], (CASES,), jnp.float32) ** block_scale(keys[4], (CASES,), ((0, 8),), -0.2, 0.2)), 0.5, 2.0),
        "fault_z": jnp.clip(jnp.exp(math.log(2.0) - 1.3862944 * jax.random.uniform(keys[5], (CASES,), jnp.float32) ** block_scale(keys[5], (CASES,), ((0, 8),), -0.2, 0.2)), 0.5, 2.0),
        "boundary_send": draw_boundary_send(jax.random.fold_in(keys[12], 71), 0),
        "branch_ends": draw_branch_ends(jax.random.fold_in(keys[12], 71), 0),
        "branch_x": jnp.clip(jnp.exp(math.log(0.05) - 1.609438 * jax.random.uniform(keys[8], (NBR,), jnp.float32) ** block_scale(keys[8], (NBR,), ((0, 32),), -0.2, 0.2)), 0.01, 0.05),
        "pickup": jnp.clip(jnp.exp(math.log(1.5) - 2.014903 * jax.random.uniform(keys[9], (NBR,), jnp.float32) ** block_scale(keys[9], (NBR,), ((0, 32),), -0.2, 0.2)), 0.2, 1.5),
        "tds": jnp.clip(jnp.exp(math.log(0.5) - 2.3025851 * jax.random.uniform(keys[10], (NBR,), jnp.float32) ** block_scale(keys[10], (NBR,), ((0, 32),), -0.2, 0.2)), 0.05, 0.5),
        "curve": place_ends(jax.random.randint(keys[11], (NBR,), 0, 3), jax.random.fold_in(keys[11], 1), 0, 2).astype(jnp.int32),
    }


def relay_of(currents, pickup, tds, curve):
    factor = jnp.where(curve == 0, 0.14, jnp.where(curve == 1, 13.5, 80.0)).astype(jnp.float32)
    exponent = jnp.where(curve == 0, 0.02, jnp.where(curve == 1, 1.0, 2.0)).astype(jnp.float32)
    scaled = currents / pickup[:, None]
    powered = jnp.exp(0.5 * exponent[:, None] * jnp.log(scaled * scaled + 1e-4))
    return jnp.maximum(powered - 1.0, 0.0) / (factor * tds)[:, None]


def reference(z_columns, resident_bus, fault_col, switch_cols, tie_x, fault_z, boundary_send, branch_ends, branch_x, pickup, tds, curve):
    count_br = branch_ends.shape[0]
    owner = (jnp.arange(count_br) // BR_DEV).astype(jnp.int32)
    from_bus = owner * BUS_DEV + branch_ends[:, 0]
    to_slot = branch_ends[:, 1]
    lower_idx = jnp.clip(owner - 1, 0, N_BUS - 1)
    upper_idx = jnp.clip(owner + 1, 0, N_BUS - 1)
    low_slot = jnp.clip(to_slot - BUS_DEV, 0, HB - 1)
    high_slot = jnp.clip(to_slot - BUS_DEV - HB, 0, HB - 1)
    to_lower = lower_idx * BUS_DEV + boundary_send[lower_idx, 1, low_slot]
    to_upper = upper_idx * BUS_DEV + boundary_send[upper_idx, 0, high_slot]
    to_bus = jnp.where(to_slot < BUS_DEV, owner * BUS_DEV + to_slot, jnp.where(to_slot < BUS_DEV + HB, to_lower, to_upper))
    groups = fault_col.shape[0] // CASE_DEV
    case_ids = jnp.arange(CASE_DEV)

    def case_block(inputs):
        fault_one, switch_one, tie_one, imped_one = inputs
        fault_cols = jnp.take(z_columns, fault_one, axis=1)
        branch_diff = jnp.take(z_columns, switch_one[:, 0], axis=1) - jnp.take(z_columns, switch_one[:, 1], axis=1)
        bus_a = resident_bus[switch_one[:, 0]]
        bus_b = resident_bus[switch_one[:, 1]]
        bus_f = resident_bus[fault_one]
        g_one = branch_diff[bus_a, case_ids] - branch_diff[bus_b, case_ids]
        g_two = branch_diff[bus_f, case_ids]
        g_three = fault_cols[bus_f, case_ids]
        weight_ratio = g_two / (tie_one + g_one)
        self_z = g_three - g_two * weight_ratio
        fault_amps = 1.0 / (self_z + imped_one)
        voltage = 1.0 - (fault_cols - branch_diff * weight_ratio[None, :]) * fault_amps[None, :]
        currents = (jnp.take(voltage, from_bus, axis=0) - jnp.take(voltage, to_bus, axis=0)) / branch_x[:, None]
        return voltage, relay_of(currents, pickup, tds, curve)

    volts, relays = lax.map(case_block, (fault_col.reshape(groups, CASE_DEV), switch_cols.reshape(groups, CASE_DEV, 2), tie_x.reshape(groups, CASE_DEV), fault_z.reshape(groups, CASE_DEV)))
    voltage = jnp.transpose(volts, (1, 0, 2)).reshape(volts.shape[1], groups * CASE_DEV)
    relay_rate = jnp.transpose(relays, (1, 0, 2)).reshape(relays.shape[1], groups * CASE_DEV)
    return voltage, relay_rate, jnp.max(relay_rate, axis=1)
```

```python
import functools

import jax
import jax.numpy as jnp
from jax import lax
from jax.experimental import pallas as pl
from jax.experimental.pallas import tpu as pltpu
from jax.sharding import PartitionSpec as P

MESH = pl.DeviceIdType.MESH
F32, BF16, I32 = jnp.float32, jnp.bfloat16, jnp.int32
BUS, COLS, CASE, BR, HB, RIM = 1024, 1024, 512, 1536, 128, 256
CHUNK = 256
MIB = 1 << 20


def pieces(value):
    high = value.astype(BF16)
    rest = value - high.astype(F32)
    middle = rest.astype(BF16)
    low = (rest - middle.astype(F32)).astype(BF16)
    return high, middle, low


def onehot(mask):
    return jnp.where(mask, 1.0, 0.0)


def voltage_kernel(
    n_x,
    n_z,
    z_hbm,
    resident_ref,
    fault_ref,
    switch_ref,
    tie_ref,
    fault_z_ref,
    lists_ref,
    volt_ref,
    z_ref,
    select_ref,
    cols_ref,
    rows_out,
    rows_in,
    part_ref,
    total_ref,
    x_in,
    z_in,
    load_sem,
    halo_send,
    halo_recv,
    x_send,
    x_recv,
    z_send,
    z_recv,
):
    n_bus = n_x * n_z
    bus = lax.axis_index("bus")
    my_x, my_z = bus // n_z, bus % n_z
    upper, lower = (bus + 1) % n_bus, (bus + n_bus - 1) % n_bus
    x_peers = [((my_x + d) % n_x) * n_z + my_z for d in range(1, n_x)]
    z_peers = [my_x * n_z + (my_z + d) % n_z for d in range(1, n_z)]

    loads = []
    for i in range(BUS // CHUNK):
        rows = pl.ds(i * CHUNK, CHUNK)
        loads.append(pltpu.make_async_copy(z_hbm.at[rows], z_ref.at[rows], load_sem.at[i]))
    for i in (0, 3, 1, 2):
        loads[i].start()

    barrier = pltpu.get_barrier_semaphore()
    peers = [upper, lower] + x_peers + z_peers
    for peer in peers:
        pl.semaphore_signal(barrier, inc=1, device_id={"bus": peer}, device_id_type=MESH)

    fault = fault_ref[...]
    first, second = switch_ref[0:1, :], switch_ref[1:2, :]

    def build(i, carry):
        k = lax.broadcasted_iota(I32, (CHUNK, CASE), 0) + i * CHUNK
        rows = pl.ds(pl.multiple_of(i * CHUNK, CHUNK), CHUNK)
        select_ref[rows, 0:CASE] = onehot(k == fault).astype(BF16)
        select_ref[rows, CASE:] = (onehot(k == first) - onehot(k == second)).astype(BF16)
        return carry

    lax.fori_loop(0, COLS // CHUNK, build, 0)

    lists = lists_ref[bus]
    rim_ids = lax.broadcasted_iota(I32, (RIM, HB), 0)

    def boundary(side, start):
        chosen = onehot(rim_ids + start == lists[side : side + 1, :]).astype(BF16)
        total = None
        for piece in pieces(z_ref[start : start + RIM, :]):
            term = lax.dot_general(
                chosen, piece, (((0,), (0,)), ((), ())), preferred_element_type=F32
            )
            total = term if total is None else total + term
        rows_out[side] = total

    loads[0].wait()
    boundary(0, 0)
    loads[3].wait()
    boundary(1, BUS - RIM)
    pl.semaphore_wait(barrier, len(peers))

    def remote(src, dst, send, recv, peer):
        return pltpu.make_async_remote_copy(
            src_ref=src,
            dst_ref=dst,
            send_sem=send,
            recv_sem=recv,
            device_id={"bus": peer},
            device_id_type=MESH,
        )

    halo = [
        remote(rows_out.at[1], rows_in.at[0], halo_send.at[0], halo_recv.at[0], upper),
        remote(rows_out.at[0], rows_in.at[1], halo_send.at[1], halo_recv.at[1], lower),
    ]
    for copy in halo:
        copy.start()
    loads[1].wait()
    loads[2].wait()

    local = resident_ref[...] - bus * BUS
    column_ids = lax.broadcasted_iota(I32, (1, COLS), 1).astype(F32)
    first_f, second_f, fault_f = first.astype(F32), second.astype(F32), fault.astype(F32)

    def columns_of(value):
        stacked = jnp.concatenate(pieces(value), axis=0)
        got = jnp.dot(stacked, select_ref[...], preferred_element_type=F32)
        n = value.shape[0]
        return (got[:n] + got[n : 2 * n]) + got[2 * n :]

    def gather(i, sums):
        g1, g2, g3 = sums
        rows = pl.ds(pl.multiple_of(i * CHUNK, CHUNK), CHUNK)
        got = columns_of(z_ref[rows, :])
        cols_ref[rows, :] = got
        faults, diff = got[:, :CASE], got[:, CASE:]
        ids = lax.broadcasted_iota(I32, (CHUNK, COLS), 0) + i * CHUNK
        owner = jnp.max(jnp.where(ids == local, column_ids, -1.0), axis=1, keepdims=True)
        is_fault = owner == fault_f
        g1 = g1 + jnp.sum(
            jnp.where(owner == first_f, diff, jnp.where(owner == second_f, -diff, 0.0)),
            axis=0,
            keepdims=True,
        )
        g2 = g2 + jnp.sum(jnp.where(is_fault, diff, 0.0), axis=0, keepdims=True)
        g3 = g3 + jnp.sum(jnp.where(is_fault, faults, 0.0), axis=0, keepdims=True)
        return g1, g2, g3

    zero = jnp.zeros((1, CASE), F32)
    sums = lax.fori_loop(0, BUS // CHUNK, gather, (zero, zero, zero))
    for i in range(3):
        part_ref[:, i * CASE : (i + 1) * CASE] = sums[i]

    x_copies = [
        remote(part_ref, x_in.at[d], x_send.at[d], x_recv.at[d], x_peers[d]) for d in range(n_x - 1)
    ]
    for copy in x_copies:
        copy.start()
    for copy in x_copies:
        copy.wait_recv()
    total = part_ref[...]
    for d in range(n_x - 1):
        total = total + x_in[d]
    total_ref[...] = total
    z_copies = [
        remote(total_ref, z_in.at[d], z_send.at[d], z_recv.at[d], z_peers[d]) for d in range(n_z - 1)
    ]
    for copy in z_copies:
        copy.start()
    for copy in halo:
        copy.wait_recv()

    def gather_halo(i, carry):
        cols_ref[pl.ds(pl.multiple_of(BUS + i * HB, HB), HB), :] = columns_of(rows_in[i])
        return carry

    lax.fori_loop(0, 2, gather_halo, 0)
    for copy in z_copies:
        copy.wait_recv()
    for d in range(n_z - 1):
        total = total + z_in[d]
    g1, g2, g3 = total[:, :CASE], total[:, CASE : 2 * CASE], total[:, 2 * CASE :]
    ratio = g2 / (tie_ref[...] + g1)
    self_z = g3 - g2 * ratio
    amps = 1.0 / (self_z + fault_z_ref[...])

    def finish(i, carry):
        rows = pl.ds(pl.multiple_of(i * HB, HB), HB)
        got = cols_ref[rows, :]
        volt_ref[rows, :] = 1.0 - (got[:, :CASE] - got[:, CASE:] * ratio) * amps
        return carry

    lax.fori_loop(0, (BUS + 2 * HB) // HB, finish, 0)
    for copy in halo + x_copies + z_copies:
        copy.wait_send()


def voltages(n_x, n_z, z_columns, resident, fault, switch, tie_x, fault_z, lists):
    vmem = pl.BlockSpec(memory_space=pltpu.VMEM)
    dma = pltpu.SemaphoreType.DMA
    return pl.pallas_call(
        functools.partial(voltage_kernel, n_x, n_z),
        out_shape=jax.ShapeDtypeStruct((BUS + 2 * HB, CASE), F32),
        in_specs=[pl.BlockSpec(memory_space=pl.ANY)] + [vmem] * 6,
        out_specs=vmem,
        scratch_shapes=[
            pltpu.VMEM((BUS, COLS), F32),
            pltpu.VMEM((COLS, 2 * CASE), BF16),
            pltpu.VMEM((BUS + 2 * HB, 2 * CASE), F32),
            pltpu.VMEM((2, HB, COLS), F32),
            pltpu.VMEM((2, HB, COLS), F32),
            pltpu.VMEM((1, 3 * CASE), F32),
            pltpu.VMEM((1, 3 * CASE), F32),
            pltpu.VMEM((n_x - 1, 1, 3 * CASE), F32),
            pltpu.VMEM((n_z - 1, 1, 3 * CASE), F32),
            dma((BUS // CHUNK,)),
            dma((2,)),
            dma((2,)),
            dma((n_x - 1,)),
            dma((n_x - 1,)),
            dma((n_z - 1,)),
            dma((n_z - 1,)),
        ],
        compiler_params=pltpu.CompilerParams(
            collective_id=0, has_side_effects=True, vmem_limit_bytes=48 * MIB
        ),
        name="voltages",
    )(z_columns, resident, fault, switch, tie_x, fault_z, lists)


STEP = 512


def relay_kernel(volt_ref, ends_ref, x_ref, pickup_ref, tds_ref, curve_ref, volt_hbm, rate_ref, worst_ref, v_ref, par_ref, sem):
    step = pl.program_id(0)
    copy = pltpu.make_async_copy(volt_ref.at[pl.ds(0, BUS)], volt_hbm, sem)

    @pl.when(step == 0)
    def _():
        copy.start()

        def split(i, carry):
            rows = pl.ds(pl.multiple_of(i * HB, HB), HB)
            for j, piece in enumerate(pieces(volt_ref[rows, :])):
                v_ref[rows, j * CASE : (j + 1) * CASE] = piece
            return carry

        lax.fori_loop(0, (BUS + 2 * HB) // HB, split, 0)
        curve = curve_ref[...]
        factor = jnp.where(curve == 0, 0.14, jnp.where(curve == 1, 13.5, 80.0))
        half = jnp.where(curve == 0, 0.01, jnp.where(curve == 1, 0.5, 1.0))
        ends = ends_ref[...].astype(F32)
        rows = [
            ends[0:1],
            ends[1:2],
            1.0 / (x_ref[...] * pickup_ref[...]),
            half,
            1.0 / (factor * tds_ref[...]),
        ]
        rows = jnp.concatenate(rows + [jnp.zeros((3, BR), F32)], axis=0)
        par_ref[...] = rows.T

    branches = pl.ds(pl.multiple_of(step * STEP, STEP), STEP)
    par = par_ref[branches, :]
    ids = lax.broadcasted_iota(I32, (STEP, BUS + 2 * HB), 1)
    start, end = par[:, 0:1].astype(I32), par[:, 1:2].astype(I32)
    signs = (onehot(ids == start) - onehot(ids == end)).astype(BF16)
    got = jnp.dot(signs, v_ref[...], preferred_element_type=F32)
    drops = (got[:, :CASE] + got[:, CASE : 2 * CASE]) + got[:, 2 * CASE :]
    scaled = drops * par[:, 2:3]
    powered = jnp.exp(par[:, 3:4] * jnp.log(scaled * scaled + 0.0001))
    rate = jnp.maximum(powered - 1.0, 0.0) * par[:, 4:5]
    rate_ref[...] = rate
    tops = rate[:, 0:128]
    for j in range(1, CASE // 128):
        tops = jnp.maximum(tops, rate[:, j * 128 : (j + 1) * 128])
    worst_ref[...] = jnp.max(tops.T, axis=0, keepdims=True)

    @pl.when(step == BR // STEP - 1)
    def _():
        copy.wait()


def relays(volt, ends, branch_x, pickup, tds, curve):
    vmem = pl.BlockSpec(memory_space=pltpu.VMEM)
    return pl.pallas_call(
        relay_kernel,
        grid=(BR // STEP,),
        out_shape=(
            jax.ShapeDtypeStruct((BUS, CASE), F32),
            jax.ShapeDtypeStruct((BR, CASE), F32),
            jax.ShapeDtypeStruct((1, BR), F32),
        ),
        in_specs=[vmem] * 6,
        out_specs=(
            pl.BlockSpec(memory_space=pl.ANY),
            pl.BlockSpec((STEP, CASE), lambda i: (i, 0)),
            pl.BlockSpec((1, STEP), lambda i: (0, i)),
        ),
        scratch_shapes=[
            pltpu.VMEM((BUS + 2 * HB, 3 * CASE), BF16),
            pltpu.VMEM((BR, 8), F32),
            pltpu.SemaphoreType.DMA,
        ],
        compiler_params=pltpu.CompilerParams(
            dimension_semantics=("arbitrary",), vmem_limit_bytes=40 * MIB
        ),
        name="relays",
    )(volt, ends, branch_x, pickup, tds, curve)


def worst_kernel(n, mine_ref, out_ref, slots, send, recv):
    case = lax.axis_index("case")
    peers = [(case + d) % n for d in range(1, n)]
    barrier = pltpu.get_barrier_semaphore()
    for peer in peers:
        pl.semaphore_signal(barrier, inc=1, device_id={"case": peer}, device_id_type=MESH)
    pl.semaphore_wait(barrier, n - 1)
    copies = [
        pltpu.make_async_remote_copy(
            src_ref=mine_ref,
            dst_ref=slots.at[d],
            send_sem=send.at[d],
            recv_sem=recv.at[d],
            device_id={"case": peers[d]},
            device_id_type=MESH,
        )
        for d in range(n - 1)
    ]
    for copy in copies:
        copy.start()
    best = mine_ref[...]
    for d in range(n - 1):
        copies[d].wait_recv()
        best = jnp.maximum(best, slots[d])
    out_ref[...] = best
    for copy in copies:
        copy.wait_send()


def worst_over_cases(mine):
    n = lax.axis_size("case")
    vmem = pl.BlockSpec(memory_space=pltpu.VMEM)
    return pl.pallas_call(
        functools.partial(worst_kernel, n),
        out_shape=jax.ShapeDtypeStruct((1, BR), F32),
        in_specs=[vmem],
        out_specs=vmem,
        scratch_shapes=[
            pltpu.VMEM((n - 1, 1, BR), F32),
            pltpu.SemaphoreType.DMA((n - 1,)),
            pltpu.SemaphoreType.DMA((n - 1,)),
        ],
        compiler_params=pltpu.CompilerParams(collective_id=1, has_side_effects=True),
        name="worst",
    )(mine)


def per_device(
    z_columns,
    resident_bus,
    fault_col,
    switch_cols,
    tie_x,
    fault_z,
    boundary_send,
    branch_ends,
    branch_x,
    pickup,
    tds,
    curve,
):
    n_bus = lax.axis_size("bus")
    n_z = 8 if n_bus % 8 == 0 else 2
    row = lambda a: a.reshape(1, -1)
    volt = voltages(
        n_bus // n_z,
        n_z,
        z_columns,
        row(resident_bus),
        row(fault_col),
        switch_cols.T,
        row(tie_x),
        row(fault_z),
        boundary_send,
    )
    voltage, rate, worst = relays(
        volt, branch_ends.T, row(branch_x), row(pickup), row(tds), row(curve)
    )
    return voltage, rate, worst_over_cases(worst).reshape(BR)


def solution(mesh):
    in_specs = (
        P("bus", None),
        P(),
        P("case"),
        P("case", None),
        P("case"),
        P("case"),
        P(),
        P("bus", None),
        P("bus"),
        P("bus"),
        P("bus"),
        P("bus"),
    )
    out_specs = (P("bus", "case"), P("bus", "case"), P("bus"))
    return jax.shard_map(
        per_device, mesh=mesh, in_specs=in_specs, out_specs=out_specs, check_vma=False
    )
```

```python
import functools

import jax
import jax.numpy as jnp
from jax import lax
from jax.experimental import pallas as pl
from jax.experimental.pallas import tpu as pltpu
from jax.sharding import PartitionSpec as P

MESH = pl.DeviceIdType.MESH
F32, BF16, I32 = jnp.float32, jnp.bfloat16, jnp.int32
BUS, COLS, CASE, BR, HB, RIM = 1024, 1024, 512, 1536, 128, 256
CHUNK = 256
MIB = 1 << 20


def pieces(value):
    high = value.astype(BF16)
    rest = value - high.astype(F32)
    middle = rest.astype(BF16)
    low = (rest - middle.astype(F32)).astype(BF16)
    return high, middle, low


def in_hbm(value):
    return pltpu.with_memory_space_constraint(value, pltpu.HBM)


def onehot(mask):
    return jnp.where(mask, 1.0, 0.0)


def voltage_kernel(
    n_x,
    n_z,
    z_hbm,
    resident_hbm,
    fault_hbm,
    switch_hbm,
    tie_hbm,
    fault_z_hbm,
    lists_hbm,
    volt_ref,
    resident_ref,
    fault_ref,
    switch_ref,
    tie_ref,
    fault_z_ref,
    lists_ref,
    z_ref,
    select_ref,
    cols_ref,
    rows_out,
    rows_in,
    part_ref,
    total_ref,
    x_in,
    z_in,
    small_sem,
    load_sem,
    halo_send,
    halo_recv,
    x_send,
    x_recv,
    z_send,
    z_recv,
):
    n_bus = n_x * n_z
    bus = lax.axis_index("bus")
    my_x, my_z = bus // n_z, bus % n_z
    upper, lower = (bus + 1) % n_bus, (bus + n_bus - 1) % n_bus
    x_peers = [((my_x + d) % n_x) * n_z + my_z for d in range(1, n_x)]
    z_peers = [my_x * n_z + (my_z + d) % n_z for d in range(1, n_z)]

    small = [
        (fault_hbm, fault_ref),
        (switch_hbm, switch_ref),
        (lists_hbm.at[bus], lists_ref),
        (resident_hbm, resident_ref),
        (tie_hbm, tie_ref),
        (fault_z_hbm, fault_z_ref),
    ]
    small = [
        pltpu.make_async_copy(src, dst, small_sem.at[i]) for i, (src, dst) in enumerate(small)
    ]
    for copy in small:
        copy.start()
    loads = []
    for i in range(BUS // CHUNK):
        rows = pl.ds(i * CHUNK, CHUNK)
        loads.append(pltpu.make_async_copy(z_hbm.at[rows], z_ref.at[rows], load_sem.at[i]))
    for i in (0, 3, 1, 2):
        loads[i].start()

    barrier = pltpu.get_barrier_semaphore()
    peers = [upper, lower] + x_peers + z_peers
    for peer in peers:
        pl.semaphore_signal(barrier, inc=1, device_id={"bus": peer}, device_id_type=MESH)

    for copy in small:
        copy.wait()
    fault = fault_ref[...]
    first, second = switch_ref[0:1, :], switch_ref[1:2, :]

    def build(i, carry):
        k = lax.broadcasted_iota(I32, (CHUNK, CASE), 0) + i * CHUNK
        rows = pl.ds(pl.multiple_of(i * CHUNK, CHUNK), CHUNK)
        select_ref[rows, 0:CASE] = onehot(k == fault).astype(BF16)
        select_ref[rows, CASE:] = (onehot(k == first) - onehot(k == second)).astype(BF16)
        return carry

    lax.fori_loop(0, COLS // CHUNK, build, 0)

    lists = lists_ref[...]
    rim_ids = lax.broadcasted_iota(I32, (RIM, HB), 0)

    def boundary(side, start):
        chosen = onehot(rim_ids + start == lists[side : side + 1, :]).astype(BF16)
        total = None
        for piece in pieces(z_ref[start : start + RIM, :]):
            term = lax.dot_general(
                chosen, piece, (((0,), (0,)), ((), ())), preferred_element_type=F32
            )
            total = term if total is None else total + term
        rows_out[side] = total

    loads[0].wait()
    boundary(0, 0)
    loads[3].wait()
    boundary(1, BUS - RIM)
    pl.semaphore_wait(barrier, len(peers))

    def remote(src, dst, send, recv, peer):
        return pltpu.make_async_remote_copy(
            src_ref=src,
            dst_ref=dst,
            send_sem=send,
            recv_sem=recv,
            device_id={"bus": peer},
            device_id_type=MESH,
        )

    halo = [
        remote(rows_out.at[1], rows_in.at[0], halo_send.at[0], halo_recv.at[0], upper),
        remote(rows_out.at[0], rows_in.at[1], halo_send.at[1], halo_recv.at[1], lower),
    ]
    for copy in halo:
        copy.start()
    loads[1].wait()
    loads[2].wait()

    local = resident_ref[...] - bus * BUS
    column_ids = lax.broadcasted_iota(I32, (1, COLS), 1).astype(F32)
    first_f, second_f, fault_f = first.astype(F32), second.astype(F32), fault.astype(F32)

    def columns_of(value):
        stacked = jnp.concatenate(pieces(value), axis=0)
        got = jnp.dot(stacked, select_ref[...], preferred_element_type=F32)
        n = value.shape[0]
        return (got[:n] + got[n : 2 * n]) + got[2 * n :]

    def gather(i, sums):
        g1, g2, g3 = sums
        rows = pl.ds(pl.multiple_of(i * CHUNK, CHUNK), CHUNK)
        got = columns_of(z_ref[rows, :])
        cols_ref[rows, :] = got
        faults, diff = got[:, :CASE], got[:, CASE:]
        ids = lax.broadcasted_iota(I32, (CHUNK, COLS), 0) + i * CHUNK
        owner = jnp.max(jnp.where(ids == local, column_ids, -1.0), axis=1, keepdims=True)
        is_fault = owner == fault_f
        g1 = g1 + jnp.sum(
            jnp.where(owner == first_f, diff, jnp.where(owner == second_f, -diff, 0.0)),
            axis=0,
            keepdims=True,
        )
        g2 = g2 + jnp.sum(jnp.where(is_fault, diff, 0.0), axis=0, keepdims=True)
        g3 = g3 + jnp.sum(jnp.where(is_fault, faults, 0.0), axis=0, keepdims=True)
        return g1, g2, g3

    zero = jnp.zeros((1, CASE), F32)
    sums = lax.fori_loop(0, BUS // CHUNK, gather, (zero, zero, zero))
    for i in range(3):
        part_ref[:, i * CASE : (i + 1) * CASE] = sums[i]

    x_copies = [
        remote(part_ref, x_in.at[d], x_send.at[d], x_recv.at[d], x_peers[d]) for d in range(n_x - 1)
    ]
    for copy in x_copies:
        copy.start()
    for copy in x_copies:
        copy.wait_recv()
    total = part_ref[...]
    for d in range(n_x - 1):
        total = total + x_in[d]
    total_ref[...] = total
    z_copies = [
        remote(total_ref, z_in.at[d], z_send.at[d], z_recv.at[d], z_peers[d]) for d in range(n_z - 1)
    ]
    for copy in z_copies:
        copy.start()
    for copy in halo:
        copy.wait_recv()

    def gather_halo(i, carry):
        cols_ref[pl.ds(pl.multiple_of(BUS + i * HB, HB), HB), :] = columns_of(rows_in[i])
        return carry

    lax.fori_loop(0, 2, gather_halo, 0)
    for copy in z_copies:
        copy.wait_recv()
    for d in range(n_z - 1):
        total = total + z_in[d]
    g1, g2, g3 = total[:, :CASE], total[:, CASE : 2 * CASE], total[:, 2 * CASE :]
    ratio = g2 / (tie_ref[...] + g1)
    self_z = g3 - g2 * ratio
    amps = 1.0 / (self_z + fault_z_ref[...])

    def finish(i, carry):
        rows = pl.ds(pl.multiple_of(i * HB, HB), HB)
        got = cols_ref[rows, :]
        volt_ref[rows, :] = 1.0 - (got[:, :CASE] - got[:, CASE:] * ratio) * amps
        return carry

    lax.fori_loop(0, (BUS + 2 * HB) // HB, finish, 0)
    for copy in halo + x_copies + z_copies:
        copy.wait_send()


def voltages(n_x, n_z, z_columns, resident, fault, switch, tie_x, fault_z, lists):
    vmem = pl.BlockSpec(memory_space=pltpu.VMEM)
    dma = pltpu.SemaphoreType.DMA
    return pl.pallas_call(
        functools.partial(voltage_kernel, n_x, n_z),
        out_shape=jax.ShapeDtypeStruct((BUS + 2 * HB, CASE), F32),
        in_specs=[pl.BlockSpec(memory_space=pltpu.HBM)] * 7,
        out_specs=vmem,
        scratch_shapes=[
            pltpu.VMEM((1, COLS), I32),
            pltpu.VMEM((1, CASE), I32),
            pltpu.VMEM((2, CASE), I32),
            pltpu.VMEM((1, CASE), F32),
            pltpu.VMEM((1, CASE), F32),
            pltpu.VMEM((2, HB), I32),
            pltpu.VMEM((BUS, COLS), F32),
            pltpu.VMEM((COLS, 2 * CASE), BF16),
            pltpu.VMEM((BUS + 2 * HB, 2 * CASE), F32),
            pltpu.VMEM((2, HB, COLS), F32),
            pltpu.VMEM((2, HB, COLS), F32),
            pltpu.VMEM((1, 3 * CASE), F32),
            pltpu.VMEM((1, 3 * CASE), F32),
            pltpu.VMEM((n_x - 1, 1, 3 * CASE), F32),
            pltpu.VMEM((n_z - 1, 1, 3 * CASE), F32),
            dma((6,)),
            dma((BUS // CHUNK,)),
            dma((2,)),
            dma((2,)),
            dma((n_x - 1,)),
            dma((n_x - 1,)),
            dma((n_z - 1,)),
            dma((n_z - 1,)),
        ],
        compiler_params=pltpu.CompilerParams(
            collective_id=0, has_side_effects=True, vmem_limit_bytes=48 * MIB
        ),
        name="voltages",
    )(*map(in_hbm, (z_columns, resident, fault, switch, tie_x, fault_z, lists)))


STEP = 512


def relay_kernel(
    volt_ref,
    ends_hbm,
    x_hbm,
    pickup_hbm,
    tds_hbm,
    curve_hbm,
    volt_hbm,
    rate_ref,
    worst_ref,
    v_ref,
    par_ref,
    ends_ref,
    x_ref,
    pickup_ref,
    tds_ref,
    curve_ref,
    sem,
    small_sem,
):
    step = pl.program_id(0)
    copy = pltpu.make_async_copy(volt_ref.at[pl.ds(0, BUS)], volt_hbm, sem)

    @pl.when(step == 0)
    def _():
        copy.start()
        small = [
            (ends_hbm, ends_ref),
            (x_hbm, x_ref),
            (pickup_hbm, pickup_ref),
            (tds_hbm, tds_ref),
            (curve_hbm, curve_ref),
        ]
        small = [
            pltpu.make_async_copy(src, dst, small_sem.at[i]) for i, (src, dst) in enumerate(small)
        ]
        for load in small:
            load.start()

        def split(i, carry):
            rows = pl.ds(pl.multiple_of(i * HB, HB), HB)
            for j, piece in enumerate(pieces(volt_ref[rows, :])):
                v_ref[rows, j * CASE : (j + 1) * CASE] = piece
            return carry

        lax.fori_loop(0, (BUS + 2 * HB) // HB, split, 0)
        for load in small:
            load.wait()
        row = lambda ref: ref[...].reshape(1, BR)
        curve = row(curve_ref)
        factor = jnp.where(curve == 0, 0.14, jnp.where(curve == 1, 13.5, 80.0))
        half = jnp.where(curve == 0, 0.01, jnp.where(curve == 1, 0.5, 1.0))
        ends = ends_ref[...].astype(F32)
        rows = [
            ends[0:1],
            ends[1:2],
            1.0 / (row(x_ref) * row(pickup_ref)),
            half,
            1.0 / (factor * row(tds_ref)),
        ]
        rows = jnp.concatenate(rows + [jnp.zeros((3, BR), F32)], axis=0)
        par_ref[...] = rows.T

    branches = pl.ds(pl.multiple_of(step * STEP, STEP), STEP)
    par = par_ref[branches, :]
    ids = lax.broadcasted_iota(I32, (STEP, BUS + 2 * HB), 1)
    start, end = par[:, 0:1].astype(I32), par[:, 1:2].astype(I32)
    signs = (onehot(ids == start) - onehot(ids == end)).astype(BF16)
    got = jnp.dot(signs, v_ref[...], preferred_element_type=F32)
    drops = (got[:, :CASE] + got[:, CASE : 2 * CASE]) + got[:, 2 * CASE :]
    scaled = drops * par[:, 2:3]
    powered = jnp.exp(par[:, 3:4] * jnp.log(scaled * scaled + 0.0001))
    rate = jnp.maximum(powered - 1.0, 0.0) * par[:, 4:5]
    rate_ref[...] = rate
    tops = rate[:, 0:128]
    for j in range(1, CASE // 128):
        tops = jnp.maximum(tops, rate[:, j * 128 : (j + 1) * 128])
    for j in range(STEP // 128):
        block = tops[j * 128 : (j + 1) * 128].T
        worst_ref[pl.ds(step * (STEP // 128) + j, 1), :] = jnp.max(block, axis=0, keepdims=True)

    @pl.when(step == BR // STEP - 1)
    def _():
        copy.wait()


def relays(volt, ends, branch_x, pickup, tds, curve):
    vmem = pl.BlockSpec(memory_space=pltpu.VMEM)
    return pl.pallas_call(
        relay_kernel,
        grid=(BR // STEP,),
        out_shape=(
            jax.ShapeDtypeStruct((BUS, CASE), F32),
            jax.ShapeDtypeStruct((BR, CASE), F32),
            jax.ShapeDtypeStruct((BR // 128, 128), F32),
        ),
        in_specs=[vmem] + [pl.BlockSpec(memory_space=pltpu.HBM)] * 5,
        out_specs=(
            pl.BlockSpec(memory_space=pltpu.HBM),
            pl.BlockSpec((STEP, CASE), lambda i: (i, 0)),
            pl.BlockSpec((BR // 128, 128), lambda i: (0, 0)),
        ),
        scratch_shapes=[
            pltpu.VMEM((BUS + 2 * HB, 3 * CASE), BF16),
            pltpu.VMEM((BR, 8), F32),
            pltpu.VMEM((2, BR), I32),
            pltpu.VMEM((BR,), F32),
            pltpu.VMEM((BR,), F32),
            pltpu.VMEM((BR,), F32),
            pltpu.VMEM((BR,), I32),
            pltpu.SemaphoreType.DMA,
            pltpu.SemaphoreType.DMA((5,)),
        ],
        compiler_params=pltpu.CompilerParams(
            dimension_semantics=("arbitrary",), vmem_limit_bytes=40 * MIB
        ),
        name="relays",
    )(volt, *map(in_hbm, (ends, branch_x, pickup, tds, curve)))


def worst_kernel(n, mine_ref, out_ref, slots, send, recv):
    case = lax.axis_index("case")
    peers = [(case + d) % n for d in range(1, n)]
    barrier = pltpu.get_barrier_semaphore()
    for peer in peers:
        pl.semaphore_signal(barrier, inc=1, device_id={"case": peer}, device_id_type=MESH)
    pl.semaphore_wait(barrier, n - 1)
    copies = [
        pltpu.make_async_remote_copy(
            src_ref=mine_ref,
            dst_ref=slots.at[d],
            send_sem=send.at[d],
            recv_sem=recv.at[d],
            device_id={"case": peers[d]},
            device_id_type=MESH,
        )
        for d in range(n - 1)
    ]
    for copy in copies:
        copy.start()
    best = mine_ref[...]
    for d in range(n - 1):
        copies[d].wait_recv()
        best = jnp.maximum(best, slots[d])
    out_ref[...] = best
    for copy in copies:
        copy.wait_send()


def worst_over_cases(mine):
    n = lax.axis_size("case")
    vmem = pl.BlockSpec(memory_space=pltpu.VMEM)
    return pl.pallas_call(
        functools.partial(worst_kernel, n),
        out_shape=jax.ShapeDtypeStruct((BR // 128, 128), F32),
        in_specs=[vmem],
        out_specs=vmem,
        scratch_shapes=[
            pltpu.VMEM((n - 1, BR // 128, 128), F32),
            pltpu.SemaphoreType.DMA((n - 1,)),
            pltpu.SemaphoreType.DMA((n - 1,)),
        ],
        compiler_params=pltpu.CompilerParams(
            collective_id=1, has_side_effects=True, vmem_limit_bytes=MIB
        ),
        name="worst",
    )(mine)


def per_device(
    z_columns,
    resident_bus,
    fault_col,
    switch_cols,
    tie_x,
    fault_z,
    boundary_send,
    branch_ends,
    branch_x,
    pickup,
    tds,
    curve,
):
    n_bus = lax.axis_size("bus")
    n_z = 8 if n_bus % 8 == 0 else 2
    row = lambda a: a.reshape(1, -1)
    volt = voltages(
        n_bus // n_z,
        n_z,
        z_columns,
        row(resident_bus),
        row(fault_col),
        switch_cols.T,
        row(tie_x),
        row(fault_z),
        boundary_send,
    )
    voltage, rate, worst = relays(
        volt, branch_ends.T, branch_x, pickup, tds, curve
    )
    return voltage, rate, worst_over_cases(worst).reshape(BR)


def solution(mesh):
    in_specs = (
        P("bus", None),
        P(),
        P("case"),
        P("case", None),
        P("case"),
        P("case"),
        P(),
        P("bus", None),
        P("bus"),
        P("bus"),
        P("bus"),
        P("bus"),
    )
    out_specs = (P("bus", "case"), P("bus", "case"), P("bus"))
    return jax.shard_map(
        per_device, mesh=mesh, in_specs=in_specs, out_specs=out_specs, check_vma=False
    )
```

```python
import functools

import jax
import jax.numpy as jnp
from jax import lax
from jax.experimental import pallas as pl
from jax.experimental.pallas import tpu as pltpu
from jax.sharding import PartitionSpec as P

MESH = pl.DeviceIdType.MESH
F32, BF16, I32 = jnp.float32, jnp.bfloat16, jnp.int32
BUS, COLS, CASE, BR, HB, RIM = 1024, 1024, 512, 1536, 128, 256
CHUNK = 256
EXT, HALF = BUS + 2 * HB, CASE // 2
MIB = 1 << 20


def pieces(value):
    high = value.astype(BF16)
    rest = value - high.astype(F32)
    middle = rest.astype(BF16)
    low = (rest - middle.astype(F32)).astype(BF16)
    return high, middle, low


def in_hbm(value):
    return pltpu.with_memory_space_constraint(value, pltpu.HBM)


def onehot(mask):
    return jnp.where(mask, 1.0, 0.0)


def relay_of(scaled, half, inverse):
    powered = jnp.exp(half * jnp.log(scaled * scaled + 0.0001))
    return jnp.maximum(powered - 1.0, 0.0) * inverse


def screen_kernel(
    n_x,
    n_z,
    n_case,
    z_hbm,
    resident_hbm,
    fault_hbm,
    switch_hbm,
    tie_hbm,
    fault_z_hbm,
    lists_hbm,
    ends_hbm,
    x_hbm,
    pickup_hbm,
    tds_hbm,
    curve_hbm,
    volt_ref,
    rate_ref,
    worst_ref,
    resident_ref,
    fault_ref,
    switch_ref,
    tie_ref,
    fault_z_ref,
    lists_ref,
    ends_ref,
    x_ref,
    pickup_ref,
    tds_ref,
    curve_ref,
    z_ref,
    select_ref,
    cols_ref,
    rows_out,
    rows_in,
    part_ref,
    total_ref,
    x_in,
    z_in,
    signs_ref,
    v_ref,
    par_ref,
    most_ref,
    most_in,
    small_sem,
    load_sem,
    halo_send,
    halo_recv,
    x_send,
    x_recv,
    z_send,
    z_recv,
    c_send,
    c_recv,
):
    n_bus = n_x * n_z
    bus, case = lax.axis_index("bus"), lax.axis_index("case")
    my_x, my_z = bus // n_z, bus % n_z
    upper, lower = (bus + 1) % n_bus, (bus + n_bus - 1) % n_bus
    x_peers = [((my_x + d) % n_x) * n_z + my_z for d in range(1, n_x)]
    z_peers = [my_x * n_z + (my_z + d) % n_z for d in range(1, n_z)]
    case_peers = [(case + d) % n_case for d in range(1, n_case)]

    small = [
        (fault_hbm, fault_ref),
        (switch_hbm, switch_ref),
        (lists_hbm.at[bus], lists_ref),
        (resident_hbm, resident_ref),
        (tie_hbm, tie_ref),
        (fault_z_hbm, fault_z_ref),
        (ends_hbm, ends_ref),
        (x_hbm, x_ref),
        (pickup_hbm, pickup_ref),
        (tds_hbm, tds_ref),
        (curve_hbm, curve_ref),
    ]
    small = [
        pltpu.make_async_copy(src, dst, small_sem.at[i]) for i, (src, dst) in enumerate(small)
    ]
    for copy in small[:4]:
        copy.start()
    loads = []
    for i in range(BUS // CHUNK):
        rows = pl.ds(i * CHUNK, CHUNK)
        loads.append(pltpu.make_async_copy(z_hbm.at[rows], z_ref.at[rows], load_sem.at[i]))
    for i in (0, 3, 1, 2):
        loads[i].start()
    for copy in small[4:]:
        copy.start()

    barrier = pltpu.get_barrier_semaphore()
    bus_peers = [upper, lower] + x_peers + z_peers
    for peer in bus_peers:
        pl.semaphore_signal(barrier, inc=1, device_id={"bus": peer}, device_id_type=MESH)
    for peer in case_peers:
        pl.semaphore_signal(barrier, inc=1, device_id={"case": peer}, device_id_type=MESH)

    for copy in small[:4]:
        copy.wait()
    fault = fault_ref[...]
    first, second = switch_ref[0:1, :], switch_ref[1:2, :]

    def build(i, carry):
        k = lax.broadcasted_iota(I32, (CHUNK, CASE), 0) + i * CHUNK
        rows = pl.ds(pl.multiple_of(i * CHUNK, CHUNK), CHUNK)
        select_ref[rows, 0:CASE] = onehot(k == fault).astype(BF16)
        select_ref[rows, CASE:] = (onehot(k == first) - onehot(k == second)).astype(BF16)
        return carry

    lax.fori_loop(0, COLS // CHUNK, build, 0)

    lists = lists_ref[...]
    rim_ids = lax.broadcasted_iota(I32, (RIM, HB), 0)

    def boundary(side, start):
        chosen = onehot(rim_ids + start == lists[side : side + 1, :]).astype(BF16)
        total = None
        for piece in pieces(z_ref[start : start + RIM, :]):
            term = lax.dot_general(
                chosen, piece, (((0,), (0,)), ((), ())), preferred_element_type=F32
            )
            total = term if total is None else total + term
        rows_out[side] = total

    loads[0].wait()
    boundary(0, 0)
    loads[3].wait()
    boundary(1, BUS - RIM)
    pl.semaphore_wait(barrier, len(bus_peers) + len(case_peers))

    def remote(src, dst, send, recv, axis, peer):
        return pltpu.make_async_remote_copy(
            src_ref=src,
            dst_ref=dst,
            send_sem=send,
            recv_sem=recv,
            device_id={axis: peer},
            device_id_type=MESH,
        )

    halo = [
        remote(rows_out.at[1], rows_in.at[0], halo_send.at[0], halo_recv.at[0], "bus", upper),
        remote(rows_out.at[0], rows_in.at[1], halo_send.at[1], halo_recv.at[1], "bus", lower),
    ]
    for copy in halo:
        copy.start()
    loads[1].wait()
    loads[2].wait()

    local = resident_ref[...] - bus * BUS
    column_ids = lax.broadcasted_iota(I32, (1, COLS), 1).astype(F32)
    first_f, second_f, fault_f = first.astype(F32), second.astype(F32), fault.astype(F32)

    def columns_of(value):
        stacked = jnp.concatenate(pieces(value), axis=0)
        got = jnp.dot(stacked, select_ref[...], preferred_element_type=F32)
        n = value.shape[0]
        return (got[:n] + got[n : 2 * n]) + got[2 * n :]

    def gather(i, sums):
        g1, g2, g3 = sums
        rows = pl.ds(pl.multiple_of(i * CHUNK, CHUNK), CHUNK)
        got = columns_of(z_ref[rows, :])
        cols_ref[rows, :] = got
        faults, diff = got[:, :CASE], got[:, CASE:]
        ids = lax.broadcasted_iota(I32, (CHUNK, COLS), 0) + i * CHUNK
        owner = jnp.max(jnp.where(ids == local, column_ids, -1.0), axis=1, keepdims=True)
        is_fault = owner == fault_f
        g1 = g1 + jnp.sum(
            jnp.where(owner == first_f, diff, jnp.where(owner == second_f, -diff, 0.0)),
            axis=0,
            keepdims=True,
        )
        g2 = g2 + jnp.sum(jnp.where(is_fault, diff, 0.0), axis=0, keepdims=True)
        g3 = g3 + jnp.sum(jnp.where(is_fault, faults, 0.0), axis=0, keepdims=True)
        return g1, g2, g3

    zero = jnp.zeros((1, CASE), F32)
    sums = lax.fori_loop(0, BUS // CHUNK, gather, (zero, zero, zero))
    for i in range(3):
        part_ref[:, i * CASE : (i + 1) * CASE] = sums[i]

    x_copies = [
        remote(part_ref, x_in.at[d], x_send.at[d], x_recv.at[d], "bus", x_peers[d])
        for d in range(n_x - 1)
    ]
    for copy in x_copies:
        copy.start()

    for copy in small[4:]:
        copy.wait()
    curve, tds = curve_ref[...], tds_ref[...]
    factor = jnp.where(curve == 0, 0.14, jnp.where(curve == 1, 13.5, 80.0))
    half = jnp.where(curve == 0, 0.01, jnp.where(curve == 1, 0.5, 1.0))
    scale = 1.0 / (x_ref[...] * pickup_ref[...])
    inverse = 1.0 / (factor * tds)

    def as_row(value):
        return jnp.concatenate([value[j : j + 1, :] for j in range(BR // 128)], axis=1)

    ends = ends_ref[...].astype(F32)
    rows = [ends[0:1], ends[1:2], as_row(scale), as_row(half), as_row(inverse)]
    rows = jnp.concatenate(rows + [jnp.zeros((3, BR), F32)], axis=0)
    par_ref[...] = rows.T

    def build_signs(i, carry):
        rows = pl.ds(pl.multiple_of(i * CHUNK, CHUNK), CHUNK)
        par = par_ref[rows, :]
        ids = lax.broadcasted_iota(I32, (CHUNK, EXT), 1)
        start, end = par[:, 0:1].astype(I32), par[:, 1:2].astype(I32)
        signs_ref[rows, :] = (onehot(ids == start) - onehot(ids == end)).astype(BF16)
        return carry

    lax.fori_loop(0, 3, build_signs, 0)
    for copy in x_copies:
        copy.wait_recv()
    total = part_ref[...]
    for d in range(n_x - 1):
        total = total + x_in[d]
    total_ref[...] = total
    z_copies = [
        remote(total_ref, z_in.at[d], z_send.at[d], z_recv.at[d], "bus", z_peers[d])
        for d in range(n_z - 1)
    ]
    for copy in z_copies:
        copy.start()
    lax.fori_loop(3, BR // CHUNK, build_signs, 0)
    for copy in halo:
        copy.wait_recv()

    def gather_halo(i, carry):
        cols_ref[pl.ds(pl.multiple_of(BUS + i * HB, HB), HB), :] = columns_of(rows_in[i])
        return carry

    lax.fori_loop(0, 2, gather_halo, 0)
    for copy in z_copies:
        copy.wait_recv()
    for d in range(n_z - 1):
        total = total + z_in[d]
    g1, g2, g3 = total[:, :CASE], total[:, CASE : 2 * CASE], total[:, 2 * CASE :]
    ratio = g2 / (tie_ref[...] + g1)
    self_z = g3 - g2 * ratio
    amps = 1.0 / (self_z + fault_z_ref[...])

    def finish(i, keep):
        rows = pl.ds(pl.multiple_of(i * HB, HB), HB)
        got = cols_ref[rows, :]
        volt = 1.0 - (got[:, :CASE] - got[:, CASE:] * ratio) * amps
        if keep:
            volt_ref[rows, :] = volt
        for j, piece in enumerate(pieces(volt)):
            for h in range(2):
                at = (h * 3 + j) * HALF
                v_ref[rows, at : at + HALF] = piece[:, h * HALF : (h + 1) * HALF]

    @pl.loop(0, BUS // HB)
    def _(i):
        finish(i, True)

    @pl.loop(BUS // HB, EXT // HB)
    def _(i):
        finish(i, False)

    for h in range(2):
        got = jnp.dot(
            signs_ref[...],
            v_ref[:, h * 3 * HALF : (h + 1) * 3 * HALF],
            preferred_element_type=F32,
        )
        rate_ref[:, h * HALF : (h + 1) * HALF] = (got[:, :HALF] + got[:, HALF : 2 * HALF]) + got[
            :, 2 * HALF :
        ]

    @pl.loop(0, BR // 128)
    def _(i):
        drops = jnp.abs(rate_ref[pl.ds(pl.multiple_of(i * 128, 128), 128), :])
        tops = drops[:, 0:128]
        for j in range(1, CASE // 128):
            tops = jnp.maximum(tops, drops[:, j * 128 : (j + 1) * 128])
        most_ref[pl.ds(i, 1), :] = jnp.max(tops.T, axis=0, keepdims=True)

    c_copies = [
        remote(most_ref, most_in.at[d], c_send.at[d], c_recv.at[d], "case", case_peers[d])
        for d in range(n_case - 1)
    ]
    for copy in c_copies:
        copy.start()

    @pl.loop(0, BR // 128)
    def _(i):
        rows = pl.ds(pl.multiple_of(i * 128, 128), 128)
        par = par_ref[rows, :]
        rate_ref[rows, :] = relay_of(rate_ref[rows, :] * par[:, 2:3], par[:, 3:4], par[:, 4:5])

    most = most_ref[...]
    for d in range(n_case - 1):
        c_copies[d].wait_recv()
        most = jnp.maximum(most, most_in[d])
    worst_ref[...] = relay_of(most * scale, half, inverse)
    for copy in halo + x_copies + z_copies + c_copies:
        copy.wait_send()


def store_kernel(volt_ref, rate_ref, worst_ref, volt_hbm, rate_hbm, worst_hbm, sem):
    pairs = [(volt_ref, volt_hbm), (rate_ref, rate_hbm), (worst_ref, worst_hbm)]
    copies = [pltpu.make_async_copy(src, dst, sem.at[i]) for i, (src, dst) in enumerate(pairs)]
    for copy in copies:
        copy.start()
    for copy in copies:
        copy.wait()


def per_device(
    z_columns,
    resident_bus,
    fault_col,
    switch_cols,
    tie_x,
    fault_z,
    boundary_send,
    branch_ends,
    branch_x,
    pickup,
    tds,
    curve,
):
    n_bus, n_case = lax.axis_size("bus"), lax.axis_size("case")
    n_z = 8 if n_bus % 8 == 0 else 2
    n_x = n_bus // n_z
    row = lambda a: a.reshape(1, -1)
    tiles = lambda a: a.reshape(-1, 128)
    operands = (
        z_columns,
        row(resident_bus),
        row(fault_col),
        switch_cols.T,
        row(tie_x),
        row(fault_z),
        boundary_send,
        branch_ends.T,
        tiles(branch_x),
        tiles(pickup),
        tiles(tds),
        tiles(curve),
    )
    vmem, hbm = pl.BlockSpec(memory_space=pltpu.VMEM), pl.BlockSpec(memory_space=pltpu.HBM)
    dma = pltpu.SemaphoreType.DMA
    shapes = (
        jax.ShapeDtypeStruct((BUS, CASE), F32),
        jax.ShapeDtypeStruct((BR, CASE), F32),
        jax.ShapeDtypeStruct((BR // 128, 128), F32),
    )
    results = pl.pallas_call(
        functools.partial(screen_kernel, n_x, n_z, n_case),
        out_shape=shapes,
        in_specs=[hbm] * len(operands),
        out_specs=(vmem,) * 3,
        scratch_shapes=[
            pltpu.VMEM((1, COLS), I32),
            pltpu.VMEM((1, CASE), I32),
            pltpu.VMEM((2, CASE), I32),
            pltpu.VMEM((1, CASE), F32),
            pltpu.VMEM((1, CASE), F32),
            pltpu.VMEM((2, HB), I32),
            pltpu.VMEM((2, BR), I32),
            pltpu.VMEM((BR // 128, 128), F32),
            pltpu.VMEM((BR // 128, 128), F32),
            pltpu.VMEM((BR // 128, 128), F32),
            pltpu.VMEM((BR // 128, 128), I32),
            pltpu.VMEM((BUS, COLS), F32),
            pltpu.VMEM((COLS, 2 * CASE), BF16),
            pltpu.VMEM((EXT, 2 * CASE), F32),
            pltpu.VMEM((2, HB, COLS), F32),
            pltpu.VMEM((2, HB, COLS), F32),
            pltpu.VMEM((1, 3 * CASE), F32),
            pltpu.VMEM((1, 3 * CASE), F32),
            pltpu.VMEM((n_x - 1, 1, 3 * CASE), F32),
            pltpu.VMEM((n_z - 1, 1, 3 * CASE), F32),
            pltpu.VMEM((BR, EXT), BF16),
            pltpu.VMEM((EXT, 3 * CASE), BF16),
            pltpu.VMEM((BR, 8), F32),
            pltpu.VMEM((BR // 128, 128), F32),
            pltpu.VMEM((n_case - 1, BR // 128, 128), F32),
            dma((11,)),
            dma((BUS // CHUNK,)),
            dma((2,)),
            dma((2,)),
            dma((n_x - 1,)),
            dma((n_x - 1,)),
            dma((n_z - 1,)),
            dma((n_z - 1,)),
            dma((n_case - 1,)),
            dma((n_case - 1,)),
        ],
        compiler_params=pltpu.CompilerParams(
            collective_id=0, has_side_effects=True, vmem_limit_bytes=44 * MIB
        ),
        name="screen",
    )(*map(in_hbm, operands))
    voltage, rate, worst = pl.pallas_call(
        store_kernel,
        out_shape=shapes,
        in_specs=[vmem] * 3,
        out_specs=(hbm,) * 3,
        scratch_shapes=[dma((3,))],
        compiler_params=pltpu.CompilerParams(vmem_limit_bytes=MIB),
        name="store",
    )(*results)
    return voltage, rate, worst.reshape(BR)


def solution(mesh):
    in_specs = (
        P("bus", None),
        P(),
        P("case"),
        P("case", None),
        P("case"),
        P("case"),
        P(),
        P("bus", None),
        P("bus"),
        P("bus"),
        P("bus"),
        P("bus"),
    )
    out_specs = (P("bus", "case"), P("bus", "case"), P("bus"))
    return jax.shard_map(
        per_device, mesh=mesh, in_specs=in_specs, out_specs=out_specs, check_vma=False
    )
```

```python
import functools

import jax
import jax.numpy as jnp
from jax import lax
from jax.experimental import pallas as pl
from jax.experimental.pallas import tpu as pltpu
from jax.sharding import PartitionSpec as P

MESH = pl.DeviceIdType.MESH
F32, BF16, I32 = jnp.float32, jnp.bfloat16, jnp.int32
BUS, COLS, CASE, BR, HB, RIM = 1024, 1024, 512, 1536, 128, 256
CHUNK = 256
EXT, HALF = BUS + 2 * HB, HB // 2
MIB = 1 << 20


def pieces(value):
    high = value.astype(BF16)
    rest = value - high.astype(F32)
    middle = rest.astype(BF16)
    low = (rest - middle.astype(F32)).astype(BF16)
    return high, middle, low


def in_hbm(value):
    return pltpu.with_memory_space_constraint(value, pltpu.HBM)


def onehot(mask):
    return jnp.where(mask, 1.0, 0.0)


def relay_of(scaled, half, inverse):
    powered = jnp.exp(half * jnp.log(scaled * scaled + 0.0001))
    return jnp.maximum(powered - 1.0, 0.0) * inverse


def screen_kernel(
    n_x,
    n_z,
    n_case,
    z_hbm,
    resident_hbm,
    fault_hbm,
    switch_hbm,
    tie_hbm,
    fault_z_hbm,
    lists_hbm,
    ends_hbm,
    x_hbm,
    pickup_hbm,
    tds_hbm,
    curve_hbm,
    volt_ref,
    rate_ref,
    worst_ref,
    resident_ref,
    fault_ref,
    switch_ref,
    tie_ref,
    fault_z_ref,
    lists_ref,
    ends_ref,
    x_ref,
    pickup_ref,
    tds_ref,
    curve_ref,
    z_ref,
    cut_ref,
    select_ref,
    cols_ref,
    rows_out,
    rows_in,
    part_ref,
    total_ref,
    x_in,
    z_in,
    signs_ref,
    v_ref,
    par_ref,
    most_ref,
    most_in,
    small_sem,
    load_sem,
    halo_send,
    halo_recv,
    hand_send,
    hand_recv,
    x_send,
    x_recv,
    z_send,
    z_recv,
    c_send,
    c_recv,
):
    n_bus = n_x * n_z
    bus, case = lax.axis_index("bus"), lax.axis_index("case")
    my_x, my_z = bus // n_z, bus % n_z
    upper, lower = (bus + 1) % n_bus, (bus + n_bus - 1) % n_bus
    x_peers = [((my_x + d) % n_x) * n_z + my_z for d in range(1, n_x)]
    z_peers = [my_x * n_z + (my_z + d) % n_z for d in range(1, n_z)]
    core = case % 2
    sibling = case + 1 - 2 * core
    case_peers = [(case + d) % n_case for d in range(1, n_case)]

    small = [
        (fault_hbm, fault_ref),
        (switch_hbm, switch_ref),
        (lists_hbm.at[bus], lists_ref),
        (resident_hbm, resident_ref),
        (tie_hbm, tie_ref),
        (fault_z_hbm, fault_z_ref),
        (ends_hbm, ends_ref),
        (x_hbm, x_ref),
        (pickup_hbm, pickup_ref),
        (tds_hbm, tds_ref),
        (curve_hbm, curve_ref),
    ]
    small = [
        pltpu.make_async_copy(src, dst, small_sem.at[i]) for i, (src, dst) in enumerate(small)
    ]
    for copy in small[:4]:
        copy.start()
    loads = []
    for i in range(BUS // CHUNK):
        rows = pl.ds(i * CHUNK, CHUNK)
        loads.append(pltpu.make_async_copy(z_hbm.at[rows], z_ref.at[rows], load_sem.at[i]))
    for i in (0, 3, 1, 2):
        loads[i].start()
    for copy in small[4:]:
        copy.start()

    barrier = pltpu.get_barrier_semaphore()
    bus_peers = [upper, lower] + x_peers + z_peers
    for peer in bus_peers:
        pl.semaphore_signal(barrier, inc=1, device_id={"bus": peer}, device_id_type=MESH)
    for peer in case_peers:
        pl.semaphore_signal(barrier, inc=1, device_id={"case": peer}, device_id_type=MESH)

    for copy in small[:4]:
        copy.wait()
    fault = fault_ref[...]
    first, second = switch_ref[0:1, :], switch_ref[1:2, :]

    def build(i, carry):
        k = lax.broadcasted_iota(I32, (CHUNK, CASE), 0) + i * CHUNK
        rows = pl.ds(pl.multiple_of(i * CHUNK, CHUNK), CHUNK)
        select_ref[rows, 0:CASE] = onehot(k == fault).astype(BF16)
        select_ref[rows, CASE:] = (onehot(k == first) - onehot(k == second)).astype(BF16)
        return carry

    lax.fori_loop(0, COLS // CHUNK, build, 0)

    lists = jnp.where(core == 0, lists_ref[:, :HALF], lists_ref[:, HALF:])
    rim_ids = lax.broadcasted_iota(I32, (RIM, HALF), 0)

    def boundary(side, start):
        chosen = onehot(rim_ids + start == lists[side : side + 1, :]).astype(BF16)
        total = None
        for piece in pieces(z_ref[start : start + RIM, :]):
            term = lax.dot_general(
                chosen, piece, (((0,), (0,)), ((), ())), preferred_element_type=F32
            )
            total = term if total is None else total + term
        rows_out[side] = total

    def remote(src, dst, send, recv, axis, peer):
        return pltpu.make_async_remote_copy(
            src_ref=src,
            dst_ref=dst,
            send_sem=send,
            recv_sem=recv,
            device_id={axis: peer},
            device_id_type=MESH,
        )

    mine = pl.ds(pl.multiple_of(core * HALF, HALF), HALF)
    halo, hand = [], []
    for side, peer in ((0, upper), (1, lower)):
        part = rows_in.at[side, mine]
        halo.append(
            remote(
                rows_out.at[1 - side], part, halo_send.at[side], halo_recv.at[side], "bus", peer
            )
        )
        hand.append(remote(part, part, hand_send.at[side], hand_recv.at[side], "case", sibling))
    local = resident_ref[...] - bus * BUS
    column_ids = lax.broadcasted_iota(I32, (1, COLS), 1).astype(F32)
    first_f, second_f, fault_f = first.astype(F32), second.astype(F32), fault.astype(F32)

    def gather(values, select):
        total = None
        for value in values:
            term = jnp.dot(value, select, preferred_element_type=F32)
            total = term if total is None else total + term
        return total

    def switch_part(i, sums):
        g1, g2, own = sums
        rows = pl.ds(i * CHUNK, CHUNK)
        z = z_ref[rows, :]
        parts = pieces(z)
        for j in range(3):
            cut_ref[j, rows, :] = parts[j]
        diff = gather(parts, select_ref[:, CASE:])
        cols_ref[rows, CASE:] = diff
        ids = lax.broadcasted_iota(I32, (CHUNK, COLS), 0) + i * CHUNK
        resident = ids == local
        owner = jnp.max(jnp.where(resident, column_ids, -1.0), axis=1, keepdims=True)
        g1 = g1 + jnp.sum(
            jnp.where(owner == first_f, diff, jnp.where(owner == second_f, -diff, 0.0)),
            axis=0,
            keepdims=True,
        )
        g2 = g2 + jnp.sum(jnp.where(owner == fault_f, diff, 0.0), axis=0, keepdims=True)
        own = own + jnp.sum(jnp.where(resident, z, 0.0), axis=0, keepdims=True)
        return g1, g2, own

    def fault_part(i):
        rows = pl.ds(i * CHUNK, CHUNK)
        parts = [cut_ref[j, rows, :] for j in range(3)]
        cols_ref[rows, :CASE] = gather(parts, select_ref[:, :CASE])

    zero = jnp.zeros((1, CASE), F32)
    sums = (zero, zero, jnp.zeros((1, COLS), F32))
    loads[0].wait()
    loads[3].wait()
    boundary(0, 0)
    boundary(1, BUS - RIM)
    sums = switch_part(0, sums)
    pl.semaphore_wait(barrier, len(bus_peers) + len(case_peers))
    for copy in halo:
        copy.start()
    loads[1].wait()
    loads[2].wait()
    for i in (3, 1, 2):
        sums = switch_part(i, sums)
    g1, g2, own = sums
    parts = pieces(jnp.broadcast_to(own, (8, COLS)))
    g3 = gather(parts, select_ref[:, :CASE])[0:1]
    for i, value in enumerate((g1, g2, g3)):
        part_ref[:, i * CASE : (i + 1) * CASE] = value

    x_copies = [
        remote(part_ref, x_in.at[d], x_send.at[d], x_recv.at[d], "bus", x_peers[d])
        for d in range(n_x - 1)
    ]
    for copy in x_copies:
        copy.start()

    for copy in small[4:]:
        copy.wait()
    curve, tds = curve_ref[...], tds_ref[...]
    factor = jnp.where(curve == 0, 0.14, jnp.where(curve == 1, 13.5, 80.0))
    half = jnp.where(curve == 0, 0.01, jnp.where(curve == 1, 0.5, 1.0))
    scale = 1.0 / (x_ref[...] * pickup_ref[...])
    inverse = 1.0 / (factor * tds)

    def as_row(value):
        return jnp.concatenate([value[j : j + 1, :] for j in range(BR // 128)], axis=1)

    ends = ends_ref[...].astype(F32)
    rows = [ends[0:1], ends[1:2], as_row(scale), as_row(half), as_row(inverse)]
    rows = jnp.concatenate(rows + [jnp.zeros((3, BR), F32)], axis=0)
    par_ref[...] = rows.T

    def build_signs(i, carry):
        rows = pl.ds(pl.multiple_of(i * CHUNK, CHUNK), CHUNK)
        par = par_ref[rows, :]
        ids = lax.broadcasted_iota(I32, (CHUNK, EXT), 1)
        start, end = par[:, 0:1].astype(I32), par[:, 1:2].astype(I32)
        signs_ref[rows, :] = (onehot(ids == start) - onehot(ids == end)).astype(BF16)
        return carry

    lax.fori_loop(0, BR // CHUNK, build_signs, 0)
    fault_part(0)
    for copy in x_copies:
        copy.wait_recv()
    total = part_ref[...]
    for d in range(n_x - 1):
        total = total + x_in[d]
    total_ref[...] = total
    z_copies = [
        remote(total_ref, z_in.at[d], z_send.at[d], z_recv.at[d], "bus", z_peers[d])
        for d in range(n_z - 1)
    ]
    for copy in z_copies:
        copy.start()
    for copy in halo:
        copy.wait_recv()
    for copy in hand:
        copy.start()
    for i in range(1, BUS // CHUNK):
        fault_part(i)
    for copy in hand:
        copy.wait_recv()
    parts = pieces(rows_in[...].reshape(2 * HB, COLS))
    cols_ref[BUS:, :] = gather(parts, select_ref[...])
    for copy in z_copies:
        copy.wait_recv()
    for d in range(n_z - 1):
        total = total + z_in[d]
    g1, g2, g3 = total[:, :CASE], total[:, CASE : 2 * CASE], total[:, 2 * CASE :]
    ratio = g2 / (tie_ref[...] + g1)
    self_z = g3 - g2 * ratio
    amps = 1.0 / (self_z + fault_z_ref[...])

    def finish(i, keep):
        rows = pl.ds(pl.multiple_of(i * HB, HB), HB)
        got = cols_ref[rows, :]
        volt = 1.0 - (got[:, :CASE] - got[:, CASE:] * ratio) * amps
        if keep:
            volt_ref[rows, :] = volt
        for j, piece in enumerate(pieces(volt)):
            v_ref[rows, j * CASE : (j + 1) * CASE] = piece

    @pl.loop(0, BUS // HB)
    def _(i):
        finish(i, True)

    @pl.loop(BUS // HB, EXT // HB)
    def _(i):
        finish(i, False)

    for i in range(BR // CHUNK):
        signs = signs_ref[i * CHUNK : (i + 1) * CHUNK, :]
        drops = None
        for j in range(3):
            term = jnp.dot(
                signs, v_ref[:, j * CASE : (j + 1) * CASE], preferred_element_type=F32
            )
            drops = term if drops is None else drops + term
        rate_ref[i * CHUNK : (i + 1) * CHUNK, :] = drops
        sizes = jnp.abs(drops)
        tops = sizes[:, 0:128]
        for j in range(1, CASE // 128):
            tops = jnp.maximum(tops, sizes[:, j * 128 : (j + 1) * 128])
        for j in range(CHUNK // 128):
            at = i * (CHUNK // 128) + j
            block = tops[j * 128 : (j + 1) * 128].T
            most_ref[at : at + 1, :] = jnp.max(block, axis=0, keepdims=True)

    c_copies = [
        remote(most_ref, most_in.at[d], c_send.at[d], c_recv.at[d], "case", case_peers[d])
        for d in range(n_case - 1)
    ]
    for copy in c_copies:
        copy.start()

    @pl.loop(0, BR // 128)
    def _(i):
        rows = pl.ds(pl.multiple_of(i * 128, 128), 128)
        par = par_ref[rows, :]
        rate_ref[rows, :] = relay_of(rate_ref[rows, :] * par[:, 2:3], par[:, 3:4], par[:, 4:5])

    most = most_ref[...]
    for d in range(n_case - 1):
        c_copies[d].wait_recv()
        most = jnp.maximum(most, most_in[d])
    worst_ref[...] = relay_of(most * scale, half, inverse)
    for copy in halo + hand + x_copies + z_copies + c_copies:
        copy.wait_send()


def store_kernel(volt_ref, rate_ref, worst_ref, volt_hbm, rate_hbm, worst_hbm, sem):
    pairs = [(worst_ref, worst_hbm)]
    for src, dst, n in ((rate_ref, rate_hbm, BR), (volt_ref, volt_hbm, BUS)):
        for i in range(n // CHUNK):
            rows = pl.ds(i * CHUNK, CHUNK)
            pairs.append((src.at[rows], dst.at[rows]))
    copies = [pltpu.make_async_copy(src, dst, sem.at[i]) for i, (src, dst) in enumerate(pairs)]
    for copy in copies:
        copy.start()
    for copy in copies:
        copy.wait()


def per_device(
    z_columns,
    resident_bus,
    fault_col,
    switch_cols,
    tie_x,
    fault_z,
    boundary_send,
    branch_ends,
    branch_x,
    pickup,
    tds,
    curve,
):
    n_bus, n_case = lax.axis_size("bus"), lax.axis_size("case")
    n_z = 8 if n_bus % 8 == 0 else 2
    n_x = n_bus // n_z
    row = lambda a: a.reshape(1, -1)
    tiles = lambda a: a.reshape(-1, 128)
    operands = (
        z_columns,
        row(resident_bus),
        row(fault_col),
        switch_cols.T,
        row(tie_x),
        row(fault_z),
        boundary_send,
        branch_ends.T,
        tiles(branch_x),
        tiles(pickup),
        tiles(tds),
        tiles(curve),
    )
    vmem, hbm = pl.BlockSpec(memory_space=pltpu.VMEM), pl.BlockSpec(memory_space=pltpu.HBM)
    dma = pltpu.SemaphoreType.DMA
    shapes = (
        jax.ShapeDtypeStruct((BUS, CASE), F32),
        jax.ShapeDtypeStruct((BR, CASE), F32),
        jax.ShapeDtypeStruct((BR // 128, 128), F32),
    )
    results = pl.pallas_call(
        functools.partial(screen_kernel, n_x, n_z, n_case),
        out_shape=shapes,
        in_specs=[hbm] * len(operands),
        out_specs=(vmem,) * 3,
        scratch_shapes=[
            pltpu.VMEM((1, COLS), I32),
            pltpu.VMEM((1, CASE), I32),
            pltpu.VMEM((2, CASE), I32),
            pltpu.VMEM((1, CASE), F32),
            pltpu.VMEM((1, CASE), F32),
            pltpu.VMEM((2, HB), I32),
            pltpu.VMEM((2, BR), I32),
            pltpu.VMEM((BR // 128, 128), F32),
            pltpu.VMEM((BR // 128, 128), F32),
            pltpu.VMEM((BR // 128, 128), F32),
            pltpu.VMEM((BR // 128, 128), I32),
            pltpu.VMEM((BUS, COLS), F32),
            pltpu.VMEM((3, BUS, COLS), BF16),
            pltpu.VMEM((COLS, 2 * CASE), BF16),
            pltpu.VMEM((EXT, 2 * CASE), F32),
            pltpu.VMEM((2, HALF, COLS), F32),
            pltpu.VMEM((2, HB, COLS), F32),
            pltpu.VMEM((1, 3 * CASE), F32),
            pltpu.VMEM((1, 3 * CASE), F32),
            pltpu.VMEM((n_x - 1, 1, 3 * CASE), F32),
            pltpu.VMEM((n_z - 1, 1, 3 * CASE), F32),
            pltpu.VMEM((BR, EXT), BF16),
            pltpu.VMEM((EXT, 3 * CASE), BF16),
            pltpu.VMEM((BR, 8), F32),
            pltpu.VMEM((BR // 128, 128), F32),
            pltpu.VMEM((n_case - 1, BR // 128, 128), F32),
            dma((11,)),
            dma((BUS // CHUNK,)),
            dma((2,)),
            dma((2,)),
            dma((2,)),
            dma((2,)),
            dma((n_x - 1,)),
            dma((n_x - 1,)),
            dma((n_z - 1,)),
            dma((n_z - 1,)),
            dma((n_case - 1,)),
            dma((n_case - 1,)),
        ],
        compiler_params=pltpu.CompilerParams(
            collective_id=0, has_side_effects=True, vmem_limit_bytes=44 * MIB
        ),
        name="screen",
    )(*map(in_hbm, operands))
    voltage, rate, worst = pl.pallas_call(
        store_kernel,
        out_shape=shapes,
        in_specs=[vmem] * 3,
        out_specs=(hbm,) * 3,
        scratch_shapes=[dma((1 + (BR + BUS) // CHUNK,))],
        compiler_params=pltpu.CompilerParams(vmem_limit_bytes=MIB),
        name="store",
    )(*results)
    return voltage, rate, worst.reshape(BR)


def solution(mesh):
    in_specs = (
        P("bus", None),
        P(),
        P("case"),
        P("case", None),
        P("case"),
        P("case"),
        P(),
        P("bus", None),
        P("bus"),
        P("bus"),
        P("bus"),
        P("bus"),
    )
    out_specs = (P("bus", "case"), P("bus", "case"), P("bus"))
    return jax.shard_map(
        per_device, mesh=mesh, in_specs=in_specs, out_specs=out_specs, check_vma=False
    )
```

```python
import functools

import jax
import jax.numpy as jnp
from jax import lax
from jax.experimental import pallas as pl
from jax.experimental.pallas import tpu as pltpu
from jax.sharding import PartitionSpec as P

MESH = pl.DeviceIdType.MESH
F32, BF16, I32 = jnp.float32, jnp.bfloat16, jnp.int32
BUS, COLS, CASE, BR, HB, RIM = 1024, 1024, 512, 1536, 128, 256
CHUNK = 256
EXT, HALF = BUS + 2 * HB, HB // 2
MIB = 1 << 20


def pieces(value):
    high = value.astype(BF16)
    rest = value - high.astype(F32)
    middle = rest.astype(BF16)
    low = (rest - middle.astype(F32)).astype(BF16)
    return high, middle, low


def in_hbm(value):
    return pltpu.with_memory_space_constraint(value, pltpu.HBM)


def onehot(mask):
    return jnp.where(mask, 1.0, 0.0)


def relay_of(scaled, half, inverse):
    powered = jnp.exp(half * jnp.log(scaled * scaled + 0.0001))
    return jnp.maximum(powered - 1.0, 0.0) * inverse


def screen_kernel(
    n_x,
    n_z,
    n_case,
    z_hbm,
    resident_hbm,
    fault_hbm,
    switch_hbm,
    tie_hbm,
    fault_z_hbm,
    lists_hbm,
    ends_hbm,
    x_hbm,
    pickup_hbm,
    tds_hbm,
    curve_hbm,
    volt_ref,
    rate_ref,
    worst_ref,
    resident_ref,
    fault_ref,
    switch_ref,
    tie_ref,
    fault_z_ref,
    lists_ref,
    ends_ref,
    x_ref,
    pickup_ref,
    tds_ref,
    curve_ref,
    z_ref,
    cut_ref,
    select_ref,
    cols_ref,
    rows_out,
    rows_in,
    part_ref,
    total_ref,
    x_in,
    z_in,
    signs_ref,
    v_ref,
    par_ref,
    most_ref,
    most_in,
    small_sem,
    load_sem,
    halo_send,
    halo_recv,
    hand_send,
    hand_recv,
    x_send,
    x_recv,
    z_send,
    z_recv,
    c_send,
    c_recv,
):
    n_bus = n_x * n_z
    bus, case = lax.axis_index("bus"), lax.axis_index("case")
    my_x, my_z = bus // n_z, bus % n_z
    upper, lower = (bus + 1) % n_bus, (bus + n_bus - 1) % n_bus
    x_peers = [((my_x + d) % n_x) * n_z + my_z for d in range(1, n_x)]
    z_peers = [my_x * n_z + (my_z + d) % n_z for d in range(1, n_z)]
    core = case % 2
    sibling = case + 1 - 2 * core
    case_peers = [(case + d) % n_case for d in range(1, n_case)]

    small = [
        (fault_hbm, fault_ref),
        (switch_hbm, switch_ref),
        (lists_hbm.at[bus], lists_ref),
        (resident_hbm, resident_ref),
        (tie_hbm, tie_ref),
        (fault_z_hbm, fault_z_ref),
        (ends_hbm, ends_ref),
        (x_hbm, x_ref),
        (pickup_hbm, pickup_ref),
        (tds_hbm, tds_ref),
        (curve_hbm, curve_ref),
    ]
    small = [
        pltpu.make_async_copy(src, dst, small_sem.at[i]) for i, (src, dst) in enumerate(small)
    ]
    for copy in small[:4]:
        copy.start()
    loads = []
    for i in range(BUS // CHUNK):
        rows = pl.ds(i * CHUNK, CHUNK)
        loads.append(pltpu.make_async_copy(z_hbm.at[rows], z_ref.at[rows], load_sem.at[i]))
    for i in (0, 3, 1, 2):
        loads[i].start()
    for copy in small[4:]:
        copy.start()

    barrier = pltpu.get_barrier_semaphore()
    bus_peers = [upper, lower] + x_peers + z_peers
    for peer in bus_peers:
        pl.semaphore_signal(barrier, inc=1, device_id={"bus": peer}, device_id_type=MESH)
    for peer in case_peers:
        pl.semaphore_signal(barrier, inc=1, device_id={"case": peer}, device_id_type=MESH)

    for copy in small[:4]:
        copy.wait()
    fault = fault_ref[...]
    first, second = switch_ref[0:1, :], switch_ref[1:2, :]

    def column_rows(i):
        k = lax.broadcasted_iota(I32, (CHUNK, CASE), 0) + i * CHUNK
        return slice(i * CHUNK, (i + 1) * CHUNK), k

    for i in range(COLS // CHUNK):
        rows, k = column_rows(i)
        select_ref[rows, CASE:] = (onehot(k == first) - onehot(k == second)).astype(BF16)

    lists = jnp.where(core == 0, lists_ref[:, :HALF], lists_ref[:, HALF:])
    rim_ids = lax.broadcasted_iota(I32, (RIM, HALF), 0)

    def boundary(side, start):
        chosen = onehot(rim_ids + start == lists[side : side + 1, :]).astype(BF16)
        total = None
        for piece in pieces(z_ref[start : start + RIM, :]):
            term = lax.dot_general(
                chosen, piece, (((0,), (0,)), ((), ())), preferred_element_type=F32
            )
            total = term if total is None else total + term
        rows_out[side] = total

    loads[0].wait()
    loads[3].wait()
    boundary(0, 0)
    boundary(1, BUS - RIM)
    for i in range(COLS // CHUNK):
        rows, k = column_rows(i)
        select_ref[rows, 0:CASE] = onehot(k == fault).astype(BF16)

    def remote(src, dst, send, recv, axis, peer):
        return pltpu.make_async_remote_copy(
            src_ref=src,
            dst_ref=dst,
            send_sem=send,
            recv_sem=recv,
            device_id={axis: peer},
            device_id_type=MESH,
        )

    halo, hand = [], []
    for side, peer in ((0, upper), (1, lower)):
        part = rows_in.at[core, side]
        halo.append(
            remote(
                rows_out.at[1 - side], part, halo_send.at[side], halo_recv.at[side], "bus", peer
            )
        )
        hand.append(remote(part, part, hand_send.at[side], hand_recv.at[side], "case", sibling))
    local = resident_ref[...] - bus * BUS
    column_ids = lax.broadcasted_iota(I32, (1, COLS), 1).astype(F32)
    first_f, second_f, fault_f = first.astype(F32), second.astype(F32), fault.astype(F32)

    def gather(values, select):
        total = None
        for value in values:
            term = jnp.dot(value, select, preferred_element_type=F32)
            total = term if total is None else total + term
        return total

    def switch_part(start, size, sums):
        g1, g2 = sums
        rows = pl.ds(start, size)
        z = z_ref[rows, :]
        parts = pieces(z)
        for j in range(3):
            cut_ref[j, rows, :] = parts[j]
        diff = gather(parts, select_ref[:, CASE:])
        cols_ref[rows, CASE:] = diff
        ids = lax.broadcasted_iota(I32, (size, COLS), 0) + start
        resident = ids == local
        owner = jnp.max(jnp.where(resident, column_ids, -1.0), axis=1, keepdims=True)
        g1 = g1 + jnp.sum(
            jnp.where(owner == first_f, diff, jnp.where(owner == second_f, -diff, 0.0)),
            axis=0,
            keepdims=True,
        )
        g2 = g2 + jnp.sum(jnp.where(owner == fault_f, diff, 0.0), axis=0, keepdims=True)
        return g1, g2

    def own_part(start, size):
        ids = lax.broadcasted_iota(I32, (size, COLS), 0) + start
        z = z_ref[pl.ds(start, size), :]
        return jnp.sum(jnp.where(ids == local, z, 0.0), axis=0, keepdims=True)

    def fault_part(i):
        rows = pl.ds(i * CHUNK, CHUNK)
        parts = [cut_ref[j, rows, :] for j in range(3)]
        cols_ref[rows, :CASE] = gather(parts, select_ref[:, :CASE])

    zero = jnp.zeros((1, CASE), F32)
    sums = (zero, zero)
    sums = switch_part(0, 128, sums)
    pl.semaphore_wait(barrier, len(bus_peers) + len(case_peers))
    for copy in halo:
        copy.start()
    loads[1].wait()
    loads[2].wait()
    own = own_part(0, 128)
    for start, size in ((128, 128), (768, 256), (256, 256)):
        sums = switch_part(start, size, sums)
        own = own + own_part(start, size)
    own = own + own_part(512, 256)
    parts = pieces(jnp.broadcast_to(own, (8, COLS)))
    g3 = gather(parts, select_ref[:, :CASE])[0:1]
    g1, g2 = switch_part(512, 256, sums)
    for i, value in enumerate((g1, g2, g3)):
        part_ref[:, i * CASE : (i + 1) * CASE] = value

    x_copies = [
        remote(part_ref, x_in.at[d], x_send.at[d], x_recv.at[d], "bus", x_peers[d])
        for d in range(n_x - 1)
    ]
    for copy in x_copies:
        copy.start()

    for copy in small[4:]:
        copy.wait()
    curve, tds = curve_ref[...], tds_ref[...]
    factor = jnp.where(curve == 0, 0.14, jnp.where(curve == 1, 13.5, 80.0))
    half = jnp.where(curve == 0, 0.01, jnp.where(curve == 1, 0.5, 1.0))
    scale = 1.0 / (x_ref[...] * pickup_ref[...])
    inverse = 1.0 / (factor * tds)

    def as_row(value):
        return jnp.concatenate([value[j : j + 1, :] for j in range(BR // 128)], axis=1)

    ends = ends_ref[...].astype(F32)
    rows = [ends[0:1], ends[1:2], as_row(scale), as_row(half), as_row(inverse)]
    rows = jnp.concatenate(rows + [jnp.zeros((3, BR), F32)], axis=0)
    par_ref[...] = rows.T

    def build_signs(i):
        rows = pl.ds(i * CHUNK, CHUNK)
        par = par_ref[rows, :]
        ids = lax.broadcasted_iota(I32, (CHUNK, EXT), 1)
        start, end = par[:, 0:1].astype(I32), par[:, 1:2].astype(I32)
        signs_ref[rows, :] = (onehot(ids == start) - onehot(ids == end)).astype(BF16)

    fault_part(0)
    build_signs(0)
    build_signs(1)
    for copy in x_copies:
        copy.wait_recv()
    total = part_ref[...]
    for d in range(n_x - 1):
        total = total + x_in[d]
    total_ref[...] = total
    z_copies = [
        remote(total_ref, z_in.at[d], z_send.at[d], z_recv.at[d], "bus", z_peers[d])
        for d in range(n_z - 1)
    ]
    for copy in z_copies:
        copy.start()
    fault_part(1)
    build_signs(2)
    build_signs(3)

    def halo_part(half):
        parts = pieces(rows_in[half].reshape(HB, COLS))
        got = gather(parts, select_ref[...])
        for side in range(2):
            at = pl.multiple_of(BUS + side * HB + half * HALF, HALF)
            cols_ref[pl.ds(at, HALF), :] = got[side * HALF : (side + 1) * HALF]

    for copy in halo:
        copy.wait_recv()
    for copy in hand:
        copy.start()
    halo_part(core)
    fault_part(2)
    build_signs(4)
    fault_part(3)
    build_signs(5)
    for copy in hand:
        copy.wait_recv()
    halo_part(1 - core)
    for copy in z_copies:
        copy.wait_recv()
    for d in range(n_z - 1):
        total = total + z_in[d]
    g1, g2, g3 = total[:, :CASE], total[:, CASE : 2 * CASE], total[:, 2 * CASE :]
    ratio = g2 / (tie_ref[...] + g1)
    self_z = g3 - g2 * ratio
    amps = 1.0 / (self_z + fault_z_ref[...])

    for i in range(EXT // HB):
        rows = slice(i * HB, (i + 1) * HB)
        volt = 1.0 - (cols_ref[rows, :CASE] - cols_ref[rows, CASE:] * ratio) * amps
        if i < BUS // HB:
            volt_ref[rows, :] = volt
        for j, piece in enumerate(pieces(volt)):
            v_ref[rows, j * CASE : (j + 1) * CASE] = piece

    for i in range(BR // CHUNK):
        signs = signs_ref[i * CHUNK : (i + 1) * CHUNK, :]
        drops = None
        for j in range(3):
            term = jnp.dot(
                signs, v_ref[:, j * CASE : (j + 1) * CASE], preferred_element_type=F32
            )
            drops = term if drops is None else drops + term
        rate_ref[i * CHUNK : (i + 1) * CHUNK, :] = drops
        sizes = jnp.abs(drops)
        tops = sizes[:, 0:128]
        for j in range(1, CASE // 128):
            tops = jnp.maximum(tops, sizes[:, j * 128 : (j + 1) * 128])
        for j in range(CHUNK // 128):
            at = i * (CHUNK // 128) + j
            block = tops[j * 128 : (j + 1) * 128].T
            most_ref[at : at + 1, :] = jnp.max(block, axis=0, keepdims=True)

    c_copies = [
        remote(most_ref, most_in.at[d], c_send.at[d], c_recv.at[d], "case", case_peers[d])
        for d in range(n_case - 1)
    ]
    for copy in c_copies:
        copy.start()

    @pl.loop(0, BR // 128)
    def _(i):
        rows = pl.ds(pl.multiple_of(i * 128, 128), 128)
        par = par_ref[rows, :]
        rate_ref[rows, :] = relay_of(rate_ref[rows, :] * par[:, 2:3], par[:, 3:4], par[:, 4:5])

    most = most_ref[...]
    for d in range(n_case - 1):
        c_copies[d].wait_recv()
        most = jnp.maximum(most, most_in[d])
    worst_ref[...] = relay_of(most * scale, half, inverse)
    for copy in halo + hand + x_copies + z_copies + c_copies:
        copy.wait_send()


def store_kernel(volt_ref, rate_ref, worst_ref, volt_hbm, rate_hbm, worst_hbm, sem):
    pairs = [(worst_ref, worst_hbm)]
    for src, dst, n in ((rate_ref, rate_hbm, BR), (volt_ref, volt_hbm, BUS)):
        for i in range(n // CHUNK):
            rows = pl.ds(i * CHUNK, CHUNK)
            pairs.append((src.at[rows], dst.at[rows]))
    copies = [pltpu.make_async_copy(src, dst, sem.at[i]) for i, (src, dst) in enumerate(pairs)]
    for copy in copies:
        copy.start()
    for copy in copies:
        copy.wait()


def per_device(
    z_columns,
    resident_bus,
    fault_col,
    switch_cols,
    tie_x,
    fault_z,
    boundary_send,
    branch_ends,
    branch_x,
    pickup,
    tds,
    curve,
):
    n_bus, n_case = lax.axis_size("bus"), lax.axis_size("case")
    n_z = 8 if n_bus % 8 == 0 else 2
    n_x = n_bus // n_z
    row = lambda a: a.reshape(1, -1)
    tiles = lambda a: a.reshape(-1, 128)
    operands = (
        z_columns,
        row(resident_bus),
        row(fault_col),
        switch_cols.T,
        row(tie_x),
        row(fault_z),
        boundary_send,
        branch_ends.T,
        tiles(branch_x),
        tiles(pickup),
        tiles(tds),
        tiles(curve),
    )
    vmem, hbm = pl.BlockSpec(memory_space=pltpu.VMEM), pl.BlockSpec(memory_space=pltpu.HBM)
    dma = pltpu.SemaphoreType.DMA
    shapes = (
        jax.ShapeDtypeStruct((BUS, CASE), F32),
        jax.ShapeDtypeStruct((BR, CASE), F32),
        jax.ShapeDtypeStruct((BR // 128, 128), F32),
    )
    results = pl.pallas_call(
        functools.partial(screen_kernel, n_x, n_z, n_case),
        out_shape=shapes,
        in_specs=[hbm] * len(operands),
        out_specs=(vmem,) * 3,
        scratch_shapes=[
            pltpu.VMEM((1, COLS), I32),
            pltpu.VMEM((1, CASE), I32),
            pltpu.VMEM((2, CASE), I32),
            pltpu.VMEM((1, CASE), F32),
            pltpu.VMEM((1, CASE), F32),
            pltpu.VMEM((2, HB), I32),
            pltpu.VMEM((2, BR), I32),
            pltpu.VMEM((BR // 128, 128), F32),
            pltpu.VMEM((BR // 128, 128), F32),
            pltpu.VMEM((BR // 128, 128), F32),
            pltpu.VMEM((BR // 128, 128), I32),
            pltpu.VMEM((BUS, COLS), F32),
            pltpu.VMEM((3, BUS, COLS), BF16),
            pltpu.VMEM((COLS, 2 * CASE), BF16),
            pltpu.VMEM((EXT, 2 * CASE), F32),
            pltpu.VMEM((2, HALF, COLS), F32),
            pltpu.VMEM((2, 2, HALF, COLS), F32),
            pltpu.VMEM((1, 3 * CASE), F32),
            pltpu.VMEM((1, 3 * CASE), F32),
            pltpu.VMEM((n_x - 1, 1, 3 * CASE), F32),
            pltpu.VMEM((n_z - 1, 1, 3 * CASE), F32),
            pltpu.VMEM((BR, EXT), BF16),
            pltpu.VMEM((EXT, 3 * CASE), BF16),
            pltpu.VMEM((BR, 8), F32),
            pltpu.VMEM((BR // 128, 128), F32),
            pltpu.VMEM((n_case - 1, BR // 128, 128), F32),
            dma((11,)),
            dma((BUS // CHUNK,)),
            dma((2,)),
            dma((2,)),
            dma((2,)),
            dma((2,)),
            dma((n_x - 1,)),
            dma((n_x - 1,)),
            dma((n_z - 1,)),
            dma((n_z - 1,)),
            dma((n_case - 1,)),
            dma((n_case - 1,)),
        ],
        compiler_params=pltpu.CompilerParams(
            collective_id=0, has_side_effects=True, vmem_limit_bytes=44 * MIB
        ),
        name="screen",
    )(*map(in_hbm, operands))
    voltage, rate, worst = pl.pallas_call(
        store_kernel,
        out_shape=shapes,
        in_specs=[vmem] * 3,
        out_specs=(hbm,) * 3,
        scratch_shapes=[dma((1 + (BR + BUS) // CHUNK,))],
        compiler_params=pltpu.CompilerParams(vmem_limit_bytes=MIB),
        name="store",
    )(*results)
    return voltage, rate, worst.reshape(BR)


def solution(mesh):
    in_specs = (
        P("bus", None),
        P(),
        P("case"),
        P("case", None),
        P("case"),
        P("case"),
        P(),
        P("bus", None),
        P("bus"),
        P("bus"),
        P("bus"),
        P("bus"),
    )
    out_specs = (P("bus", "case"), P("bus", "case"), P("bus"))
    return jax.shard_map(
        per_device, mesh=mesh, in_specs=in_specs, out_specs=out_specs, check_vma=False
    )
```

```python
import functools

import jax
import jax.numpy as jnp
from jax import lax
from jax.experimental import pallas as pl
from jax.experimental.pallas import tpu as pltpu
from jax.sharding import PartitionSpec as P

MESH = pl.DeviceIdType.MESH
F32, BF16, I32 = jnp.float32, jnp.bfloat16, jnp.int32
BUS, COLS, CASE, BR, HB, RIM = 1024, 1024, 512, 1536, 128, 256
CHUNK = 256
EXT, HALF = BUS + 2 * HB, HB // 2
MIB = 1 << 20


def pieces(value):
    high = value.astype(BF16)
    rest = value - high.astype(F32)
    middle = rest.astype(BF16)
    low = (rest - middle.astype(F32)).astype(BF16)
    return high, middle, low


def in_hbm(value):
    return pltpu.with_memory_space_constraint(value, pltpu.HBM)


def farthest_first(n):
    return sorted(range(1, n), key=lambda d: (-min(d, n - d), d))


def onehot(mask):
    return jnp.where(mask, 1.0, 0.0)


def relay_of(scaled, half, inverse):
    powered = jnp.exp(half * jnp.log(scaled * scaled + 0.0001))
    return jnp.maximum(powered - 1.0, 0.0) * inverse


def screen_kernel(
    n_x,
    n_z,
    n_case,
    z_hbm,
    resident_hbm,
    fault_hbm,
    switch_hbm,
    tie_hbm,
    fault_z_hbm,
    lists_hbm,
    ends_hbm,
    x_hbm,
    pickup_hbm,
    tds_hbm,
    curve_hbm,
    volt_ref,
    rate_ref,
    worst_ref,
    resident_ref,
    fault_ref,
    switch_ref,
    tie_ref,
    fault_z_ref,
    lists_ref,
    ends_ref,
    x_ref,
    pickup_ref,
    tds_ref,
    curve_ref,
    z_ref,
    cut_ref,
    select_ref,
    cols_ref,
    rows_out,
    rows_in,
    part_ref,
    total_ref,
    x_in,
    z_in,
    signs_ref,
    v_ref,
    par_ref,
    most_ref,
    most_in,
    small_sem,
    load_sem,
    halo_send,
    halo_recv,
    hand_send,
    hand_recv,
    x_send,
    x_recv,
    z_send,
    z_recv,
    c_send,
    c_recv,
):
    n_bus = n_x * n_z
    bus, case = lax.axis_index("bus"), lax.axis_index("case")
    my_x, my_z = bus // n_z, bus % n_z
    upper, lower = (bus + 1) % n_bus, (bus + n_bus - 1) % n_bus
    x_peers = [((my_x + d) % n_x) * n_z + my_z for d in farthest_first(n_x)]
    z_peers = [my_x * n_z + (my_z + d) % n_z for d in farthest_first(n_z)]
    core = case % 2
    sibling = case + 1 - 2 * core
    case_peers = [(case + d) % n_case for d in farthest_first(n_case)]

    small = [
        (fault_hbm, fault_ref),
        (switch_hbm, switch_ref),
        (lists_hbm.at[bus], lists_ref),
        (resident_hbm, resident_ref),
        (tie_hbm, tie_ref),
        (fault_z_hbm, fault_z_ref),
        (ends_hbm, ends_ref),
        (x_hbm, x_ref),
        (pickup_hbm, pickup_ref),
        (tds_hbm, tds_ref),
        (curve_hbm, curve_ref),
    ]
    small = [
        pltpu.make_async_copy(src, dst, small_sem.at[i]) for i, (src, dst) in enumerate(small)
    ]
    for copy in small[:4]:
        copy.start()
    loads = []
    for i in range(BUS // CHUNK):
        rows = pl.ds(i * CHUNK, CHUNK)
        loads.append(pltpu.make_async_copy(z_hbm.at[rows], z_ref.at[rows], load_sem.at[i]))
    for i in (0, 3, 1, 2):
        loads[i].start()
    for copy in small[4:]:
        copy.start()

    barrier = pltpu.get_barrier_semaphore()
    bus_peers = [upper, lower] + x_peers + z_peers
    for peer in bus_peers:
        pl.semaphore_signal(barrier, inc=1, device_id={"bus": peer}, device_id_type=MESH)
    for peer in case_peers:
        pl.semaphore_signal(barrier, inc=1, device_id={"case": peer}, device_id_type=MESH)

    for copy in small[:4]:
        copy.wait()
    fault = fault_ref[...]
    first, second = switch_ref[0:1, :], switch_ref[1:2, :]

    def column_rows(i):
        k = lax.broadcasted_iota(I32, (CHUNK, CASE), 0) + i * CHUNK
        return slice(i * CHUNK, (i + 1) * CHUNK), k

    for i in range(COLS // CHUNK):
        rows, k = column_rows(i)
        select_ref[rows, CASE:] = (onehot(k == first) - onehot(k == second)).astype(BF16)

    lists = jnp.where(core == 0, lists_ref[:, :HALF], lists_ref[:, HALF:])
    rim_ids = lax.broadcasted_iota(I32, (RIM, HALF), 0)

    def boundary(side, start):
        chosen = onehot(rim_ids + start == lists[side : side + 1, :]).astype(BF16)
        total = None
        for piece in pieces(z_ref[start : start + RIM, :]):
            term = lax.dot_general(
                chosen, piece, (((0,), (0,)), ((), ())), preferred_element_type=F32
            )
            total = term if total is None else total + term
        rows_out[side] = total

    loads[0].wait()
    loads[3].wait()
    boundary(0, 0)
    boundary(1, BUS - RIM)
    for i in range(COLS // CHUNK):
        rows, k = column_rows(i)
        select_ref[rows, 0:CASE] = onehot(k == fault).astype(BF16)

    def remote(src, dst, send, recv, axis, peer):
        return pltpu.make_async_remote_copy(
            src_ref=src,
            dst_ref=dst,
            send_sem=send,
            recv_sem=recv,
            device_id={axis: peer},
            device_id_type=MESH,
        )

    halo, hand = [], []
    for side, peer in ((0, upper), (1, lower)):
        part = rows_in.at[core, side]
        halo.append(
            remote(
                rows_out.at[1 - side], part, halo_send.at[side], halo_recv.at[side], "bus", peer
            )
        )
        hand.append(remote(part, part, hand_send.at[side], hand_recv.at[side], "case", sibling))
    local = resident_ref[...] - bus * BUS
    column_ids = lax.broadcasted_iota(I32, (1, COLS), 1).astype(F32)
    first_f, second_f, fault_f = first.astype(F32), second.astype(F32), fault.astype(F32)

    def gather(values, select):
        total = None
        for value in values:
            term = jnp.dot(value, select, preferred_element_type=F32)
            total = term if total is None else total + term
        return total

    def switch_part(start, size, sums):
        g1, g2 = sums
        rows = pl.ds(start, size)
        z = z_ref[rows, :]
        parts = pieces(z)
        for j in range(3):
            cut_ref[j, rows, :] = parts[j]
        diff = gather(parts, select_ref[:, CASE:])
        cols_ref[rows, CASE:] = diff
        ids = lax.broadcasted_iota(I32, (size, COLS), 0) + start
        resident = ids == local
        owner = jnp.max(jnp.where(resident, column_ids, -1.0), axis=1, keepdims=True)
        g1 = g1 + jnp.sum(
            jnp.where(owner == first_f, diff, jnp.where(owner == second_f, -diff, 0.0)),
            axis=0,
            keepdims=True,
        )
        g2 = g2 + jnp.sum(jnp.where(owner == fault_f, diff, 0.0), axis=0, keepdims=True)
        return g1, g2

    def own_part(start, size):
        ids = lax.broadcasted_iota(I32, (size, COLS), 0) + start
        z = z_ref[pl.ds(start, size), :]
        return jnp.sum(jnp.where(ids == local, z, 0.0), axis=0, keepdims=True)

    def fault_part(i):
        rows = pl.ds(i * CHUNK, CHUNK)
        parts = [cut_ref[j, rows, :] for j in range(3)]
        cols_ref[rows, :CASE] = gather(parts, select_ref[:, :CASE])

    zero = jnp.zeros((1, CASE), F32)
    sums = (zero, zero)
    sums = switch_part(0, 128, sums)
    pl.semaphore_wait(barrier, len(bus_peers) + len(case_peers))
    for copy in halo:
        copy.start()
    loads[1].wait()
    loads[2].wait()
    own = own_part(0, 128)
    for start, size in ((128, 128), (768, 256), (256, 256)):
        sums = switch_part(start, size, sums)
        own = own + own_part(start, size)
    own = own + own_part(512, 256)
    parts = pieces(jnp.broadcast_to(own, (8, COLS)))
    g3 = gather(parts, select_ref[:, :CASE])[0:1]
    g1, g2 = switch_part(512, 256, sums)
    for i, value in enumerate((g1, g2, g3)):
        part_ref[:, i * CASE : (i + 1) * CASE] = value

    x_copies = [
        remote(part_ref, x_in.at[d], x_send.at[d], x_recv.at[d], "bus", x_peers[d])
        for d in range(n_x - 1)
    ]
    for copy in x_copies:
        copy.start()

    for copy in small[4:]:
        copy.wait()
    curve, tds = curve_ref[...], tds_ref[...]
    factor = jnp.where(curve == 0, 0.14, jnp.where(curve == 1, 13.5, 80.0))
    half = jnp.where(curve == 0, 0.01, jnp.where(curve == 1, 0.5, 1.0))
    scale = 1.0 / (x_ref[...] * pickup_ref[...])
    inverse = 1.0 / (factor * tds)

    def as_row(value):
        return jnp.concatenate([value[j : j + 1, :] for j in range(BR // 128)], axis=1)

    ends = ends_ref[...].astype(F32)
    rows = [ends[0:1], ends[1:2], as_row(scale), as_row(half), as_row(inverse)]
    rows = jnp.concatenate(rows + [jnp.zeros((3, BR), F32)], axis=0)
    par_ref[...] = rows.T

    def build_signs(i):
        rows = pl.ds(i * CHUNK, CHUNK)
        par = par_ref[rows, :]
        ids = lax.broadcasted_iota(I32, (CHUNK, EXT), 1)
        start, end = par[:, 0:1].astype(I32), par[:, 1:2].astype(I32)
        signs_ref[rows, :] = (onehot(ids == start) - onehot(ids == end)).astype(BF16)

    fault_part(0)
    build_signs(0)
    build_signs(1)
    for copy in x_copies:
        copy.wait_recv()
    total = part_ref[...]
    for d in range(n_x - 1):
        total = total + x_in[d]
    total_ref[...] = total
    z_copies = [
        remote(total_ref, z_in.at[d], z_send.at[d], z_recv.at[d], "bus", z_peers[d])
        for d in range(n_z - 1)
    ]
    for copy in z_copies:
        copy.start()
    fault_part(1)
    build_signs(2)
    build_signs(3)

    def halo_part(half):
        parts = pieces(rows_in[half].reshape(HB, COLS))
        got = gather(parts, select_ref[...])
        for side in range(2):
            at = pl.multiple_of(BUS + side * HB + half * HALF, HALF)
            cols_ref[pl.ds(at, HALF), :] = got[side * HALF : (side + 1) * HALF]

    for copy in halo:
        copy.wait_recv()
    for copy in hand:
        copy.start()
    halo_part(core)
    fault_part(2)
    build_signs(4)
    fault_part(3)
    build_signs(5)
    for copy in hand:
        copy.wait_recv()
    halo_part(1 - core)
    for copy in z_copies:
        copy.wait_recv()
    for d in range(n_z - 1):
        total = total + z_in[d]
    g1, g2, g3 = total[:, :CASE], total[:, CASE : 2 * CASE], total[:, 2 * CASE :]
    ratio = g2 / (tie_ref[...] + g1)
    self_z = g3 - g2 * ratio
    amps = 1.0 / (self_z + fault_z_ref[...])

    for i in range(EXT // HB):
        rows = slice(i * HB, (i + 1) * HB)
        volt = 1.0 - (cols_ref[rows, :CASE] - cols_ref[rows, CASE:] * ratio) * amps
        if i < BUS // HB:
            volt_ref[rows, :] = volt
        for j, piece in enumerate(pieces(volt)):
            v_ref[rows, j * CASE : (j + 1) * CASE] = piece

    for i in range(BR // CHUNK):
        signs = signs_ref[i * CHUNK : (i + 1) * CHUNK, :]
        drops = None
        for j in range(3):
            term = jnp.dot(
                signs, v_ref[:, j * CASE : (j + 1) * CASE], preferred_element_type=F32
            )
            drops = term if drops is None else drops + term
        rate_ref[i * CHUNK : (i + 1) * CHUNK, :] = drops
        sizes = jnp.abs(drops)
        tops = sizes[:, 0:128]
        for j in range(1, CASE // 128):
            tops = jnp.maximum(tops, sizes[:, j * 128 : (j + 1) * 128])
        for j in range(CHUNK // 128):
            at = i * (CHUNK // 128) + j
            block = tops[j * 128 : (j + 1) * 128].T
            most_ref[at : at + 1, :] = jnp.max(block, axis=0, keepdims=True)

    c_copies = [
        remote(most_ref, most_in.at[d], c_send.at[d], c_recv.at[d], "case", case_peers[d])
        for d in range(n_case - 1)
    ]
    for copy in c_copies:
        copy.start()

    @pl.loop(0, BR // 128)
    def _(i):
        rows = pl.ds(pl.multiple_of(i * 128, 128), 128)
        par = par_ref[rows, :]
        rate_ref[rows, :] = relay_of(rate_ref[rows, :] * par[:, 2:3], par[:, 3:4], par[:, 4:5])

    most = most_ref[...]
    for d in range(n_case - 1):
        c_copies[d].wait_recv()
        most = jnp.maximum(most, most_in[d])
    worst_ref[...] = relay_of(most * scale, half, inverse)
    for copy in halo + hand + x_copies + z_copies + c_copies:
        copy.wait_send()


def store_kernel(volt_ref, rate_ref, worst_ref, volt_hbm, rate_hbm, worst_hbm, sem):
    pairs = [(worst_ref, worst_hbm)]
    for src, dst, n in ((rate_ref, rate_hbm, BR), (volt_ref, volt_hbm, BUS)):
        for i in range(n // CHUNK):
            rows = pl.ds(i * CHUNK, CHUNK)
            pairs.append((src.at[rows], dst.at[rows]))
    copies = [pltpu.make_async_copy(src, dst, sem.at[i]) for i, (src, dst) in enumerate(pairs)]
    for copy in copies:
        copy.start()
    for copy in copies:
        copy.wait()


def per_device(
    z_columns,
    resident_bus,
    fault_col,
    switch_cols,
    tie_x,
    fault_z,
    boundary_send,
    branch_ends,
    branch_x,
    pickup,
    tds,
    curve,
):
    n_bus, n_case = lax.axis_size("bus"), lax.axis_size("case")
    n_z = 8 if n_bus % 8 == 0 else 2
    n_x = n_bus // n_z
    row = lambda a: a.reshape(1, -1)
    tiles = lambda a: a.reshape(-1, 128)
    operands = (
        z_columns,
        row(resident_bus),
        row(fault_col),
        switch_cols.T,
        row(tie_x),
        row(fault_z),
        boundary_send,
        branch_ends.T,
        tiles(branch_x),
        tiles(pickup),
        tiles(tds),
        tiles(curve),
    )
    vmem, hbm = pl.BlockSpec(memory_space=pltpu.VMEM), pl.BlockSpec(memory_space=pltpu.HBM)
    dma = pltpu.SemaphoreType.DMA
    shapes = (
        jax.ShapeDtypeStruct((BUS, CASE), F32),
        jax.ShapeDtypeStruct((BR, CASE), F32),
        jax.ShapeDtypeStruct((BR // 128, 128), F32),
    )
    results = pl.pallas_call(
        functools.partial(screen_kernel, n_x, n_z, n_case),
        out_shape=shapes,
        in_specs=[hbm] * len(operands),
        out_specs=(vmem,) * 3,
        scratch_shapes=[
            pltpu.VMEM((1, COLS), I32),
            pltpu.VMEM((1, CASE), I32),
            pltpu.VMEM((2, CASE), I32),
            pltpu.VMEM((1, CASE), F32),
            pltpu.VMEM((1, CASE), F32),
            pltpu.VMEM((2, HB), I32),
            pltpu.VMEM((2, BR), I32),
            pltpu.VMEM((BR // 128, 128), F32),
            pltpu.VMEM((BR // 128, 128), F32),
            pltpu.VMEM((BR // 128, 128), F32),
            pltpu.VMEM((BR // 128, 128), I32),
            pltpu.VMEM((BUS, COLS), F32),
            pltpu.VMEM((3, BUS, COLS), BF16),
            pltpu.VMEM((COLS, 2 * CASE), BF16),
            pltpu.VMEM((EXT, 2 * CASE), F32),
            pltpu.VMEM((2, HALF, COLS), F32),
            pltpu.VMEM((2, 2, HALF, COLS), F32),
            pltpu.VMEM((1, 3 * CASE), F32),
            pltpu.VMEM((1, 3 * CASE), F32),
            pltpu.VMEM((n_x - 1, 1, 3 * CASE), F32),
            pltpu.VMEM((n_z - 1, 1, 3 * CASE), F32),
            pltpu.VMEM((BR, EXT), BF16),
            pltpu.VMEM((EXT, 3 * CASE), BF16),
            pltpu.VMEM((BR, 8), F32),
            pltpu.VMEM((BR // 128, 128), F32),
            pltpu.VMEM((n_case - 1, BR // 128, 128), F32),
            dma((11,)),
            dma((BUS // CHUNK,)),
            dma((2,)),
            dma((2,)),
            dma((2,)),
            dma((2,)),
            dma((n_x - 1,)),
            dma((n_x - 1,)),
            dma((n_z - 1,)),
            dma((n_z - 1,)),
            dma((n_case - 1,)),
            dma((n_case - 1,)),
        ],
        compiler_params=pltpu.CompilerParams(
            collective_id=0, has_side_effects=True, vmem_limit_bytes=44 * MIB
        ),
        name="screen",
    )(*map(in_hbm, operands))
    voltage, rate, worst = pl.pallas_call(
        store_kernel,
        out_shape=shapes,
        in_specs=[vmem] * 3,
        out_specs=(hbm,) * 3,
        scratch_shapes=[dma((1 + (BR + BUS) // CHUNK,))],
        compiler_params=pltpu.CompilerParams(vmem_limit_bytes=MIB),
        name="store",
    )(*results)
    return voltage, rate, worst.reshape(BR)


def solution(mesh):
    in_specs = (
        P("bus", None),
        P(),
        P("case"),
        P("case", None),
        P("case"),
        P("case"),
        P(),
        P("bus", None),
        P("bus"),
        P("bus"),
        P("bus"),
        P("bus"),
    )
    out_specs = (P("bus", "case"), P("bus", "case"), P("bus"))
    return jax.shard_map(
        per_device, mesh=mesh, in_specs=in_specs, out_specs=out_specs, check_vma=False
    )
```
